512 devices in a mesh: expert: 128 (over y, x_lo, z), half: 4 (over x_hi, core).
Axes of the slice: x: 4 (x_hi: 2, x_lo: 2; x = x_hi * 2 + x_lo), y: 4, z: 16, core: 2. Of those that a mesh axis runs over, the one named last changes fastest.
Arguments:
- tokens: bfloat16 [25088, 1024], P('expert', 'half'), may hold values from -128 to 128
- slot_params: bfloat16 [1024, 256], P('half'), may hold values from -0.5 to 0.5
- w_up: bfloat16 [128, 1024, 4096], P('expert', None, 'half'), may hold values from -0.1875 to 0.1875
- w_down: bfloat16 [128, 4096, 1024], P('expert', 'half'), may hold values from -0.09375 to 0.09375
- cotangent: bfloat16 [25088, 1024], P('expert', 'half'), may hold values from -6 to 6
Outputs:
- mixed: bfloat16 [25088, 1024], P('expert', 'half')
- grad_tokens: bfloat16 [25088, 1024], P('expert', 'half')
- grad_params: float32 [1024, 256], P('half')
The draws below stay inside these ranges and needn't reach their ends.
All inputs are finite; a program needn't handle non-finite values.
Results may differ from the reference program's by a relative error of at most 0.017.
Values may be sent and summed in bfloat16 or wider, within the bound.
A program may use at most 64 MiB of HBM per device.

```python
import math
import jax
import jax.numpy as jnp
from jax import lax

D = 1024
MLP_DIM = 4096
SEQ = 196
SLOTS = 2
EXPERTS = 128
COLUMNS = 256
IMAGES = 128
TOKENS = 25088
N_HALF = 4


def shared_draw(key):
    subkeys = [jax.random.fold_in(key, 101 + offset) for offset in range(9)]
    normals = jnp.clip(jax.random.normal(subkeys[0], (D, COLUMNS), jnp.float32), -4.0, 4.0)
    column_scale = jnp.exp(jax.random.uniform(subkeys[1], (1, COLUMNS), jnp.float32, math.log(0.5), math.log(4.0)))
    slot_matrix = (normals * column_scale / math.sqrt(D)).astype(jnp.bfloat16).astype(jnp.float32)
    gaussian = jnp.clip(jax.random.normal(subkeys[2], (IMAGES, SEQ, D), jnp.float32), -5.0, 5.0)
    row_scale = jnp.exp(jax.random.uniform(subkeys[3], (IMAGES, SEQ, 1), jnp.float32, math.log(0.5), math.log(4.0)))
    image_tokens = row_scale * gaussian
    return (slot_matrix, image_tokens.reshape(TOKENS, D))


def draw_tokens(key, part):
    return shared_draw(key)[1].astype(jnp.bfloat16)


def draw_slot_params(key, part):
    return shared_draw(key)[0].astype(jnp.bfloat16)


def block_scale(rng, shape, pieces, smallest, largest):
    level, own = 1.0, jax.random.fold_in(rng, 6)
    for position, blocks in pieces:
        draws = jnp.exp(jax.random.uniform(jax.random.fold_in(own, position), (blocks,), jnp.float32, smallest / len(pieces), largest / len(pieces)))
        level = level * jnp.repeat(draws, shape[position] // blocks).reshape([-1 if axis == position else 1 for axis in range(len(shape))])
    return level


def scatter_about(key, shape, width, most, pieces=(), kind=jnp.bfloat16):
    entries = width * jax.random.normal(key, shape, jnp.float32)
    if pieces:
        entries = entries * block_scale(key, shape, pieces, -0.22, 0.18)
    return jnp.clip(entries, -most, most).astype(kind)


def setup_inputs(seed: int = 0) -> dict:
    seeds = jax.random.split(jax.random.key(seed), 6)
    return {
        "tokens": draw_tokens(jax.random.fold_in(seeds[5], 71), 0),
        "slot_params": draw_slot_params(jax.random.fold_in(seeds[5], 71), 0),
        "w_up": scatter_about(seeds[2], (EXPERTS, D, MLP_DIM), D ** -0.5, 0.1875, ((0, 128), (2, 4))),
        "w_down": scatter_about(seeds[3], (EXPERTS, MLP_DIM, D), MLP_DIM ** -0.5, 0.09375, ((0, 128), (1, 4))),
        "cotangent": scatter_about(seeds[4], (TOKENS, D), 1.0, 6.0, ((0, 128), (1, 4))),
    }


def gelu_grad(preact, upstream):
    pullback = jax.vjp(jax.nn.gelu, preact)[1]
    return pullback(upstream)[0]

def softmax_back(probabilities, upstream, over_axis):
    inner = lax.optimization_barrier(jnp.sum(probabilities * upstream, axis=over_axis, keepdims=True))
    return probabilities * (upstream - inner)

def rounded_sum(partials):
    rounded = lax.optimization_barrier(partials.astype(jnp.bfloat16))
    return lax.optimization_barrier(jnp.sum(rounded.astype(jnp.float32), axis=0)).astype(jnp.bfloat16)

def expert_rows(operands):
    slot_rows, grad_rows, up_matrix, down_matrix = operands
    block_width = MLP_DIM // N_HALF
    row_count = slot_rows.shape[0]
    up_wide = up_matrix.astype(jnp.float32)
    down_wide = down_matrix.astype(jnp.float32)
    preact = jnp.dot(slot_rows.astype(jnp.float32), up_wide)
    hidden = jax.nn.gelu(preact).astype(jnp.bfloat16)
    partial_out = jnp.einsum('rhk,hkd->hrd', hidden.astype(jnp.float32).reshape(row_count, N_HALF, block_width), down_wide.reshape(N_HALF, block_width, D))
    slot_out = rounded_sum(partial_out)
    grad_hidden = jnp.dot(grad_rows.astype(jnp.float32), down_wide.T)
    grad_preact = gelu_grad(preact, grad_hidden).astype(jnp.bfloat16)
    partial_in = jnp.einsum('rhk,dhk->hrd', grad_preact.astype(jnp.float32).reshape(row_count, N_HALF, block_width), up_wide.reshape(D, N_HALF, block_width))
    grad_slot_in = rounded_sum(partial_in)
    return (slot_out, grad_slot_in)

def to_experts(per_image):
    grouped = per_image.reshape(IMAGES, EXPERTS, SLOTS, D)
    return jnp.transpose(grouped, (1, 0, 2, 3)).reshape(EXPERTS, IMAGES * SLOTS, D)

def from_experts(per_expert):
    grouped = per_expert.reshape(EXPERTS, IMAGES, SLOTS, D)
    return jnp.transpose(grouped, (1, 0, 2, 3)).reshape(IMAGES, COLUMNS, D)

def reference(tokens, slot_params, w_up, w_down, cotangent):
    inputs = tokens.reshape(IMAGES, SEQ, D).astype(jnp.float32)
    upstream = cotangent.reshape(IMAGES, SEQ, D).astype(jnp.float32)
    params_wide = slot_params.astype(jnp.float32)
    logits = jnp.einsum('imd,dc->imc', inputs, params_wide)
    dispatch = jax.nn.softmax(logits, axis=1)
    combine = jax.nn.softmax(logits, axis=2)
    dispatch_bf = dispatch.astype(jnp.bfloat16)
    combine_bf = combine.astype(jnp.bfloat16)
    slot_in = jnp.einsum('imc,imd->icd', dispatch_bf.astype(jnp.float32), inputs).astype(jnp.bfloat16)
    grad_slot_out = jnp.einsum('imc,imd->icd', combine_bf.astype(jnp.float32), upstream).astype(jnp.bfloat16)
    expert_out, expert_grad = lax.map(expert_rows, (to_experts(slot_in), to_experts(grad_slot_out), w_up, w_down))
    slot_out = from_experts(expert_out).astype(jnp.float32)
    grad_slot_in = from_experts(expert_grad).astype(jnp.float32)
    mixed = jnp.einsum('imc,icd->imd', combine_bf.astype(jnp.float32), slot_out).astype(jnp.bfloat16)
    grad_combine = jnp.einsum('imd,icd->imc', upstream, slot_out)
    grad_dispatch = jnp.einsum('imd,icd->imc', inputs, grad_slot_in)
    grad_logits = softmax_back(combine, grad_combine, 2) + softmax_back(dispatch, grad_dispatch, 1)
    grad_logit_bf = grad_logits.astype(jnp.bfloat16).astype(jnp.float32)
    grad_tokens = jnp.einsum('imc,icd->imd', dispatch_bf.astype(jnp.float32), grad_slot_in) + jnp.einsum('imc,dc->imd', grad_logit_bf, params_wide)
    grad_params = jnp.einsum('imd,imc->dc', inputs, grad_logit_bf)
    return (mixed.reshape(TOKENS, D), grad_tokens.astype(jnp.bfloat16).reshape(TOKENS, D), grad_params)
```

```python
import jax
import jax.numpy as jnp
from jax import lax
from jax.sharding import PartitionSpec as P

SEQ = 196
SLOTS = 2
EXPERT = ("y", "x_lo", "z")
HALF = ("x_hi", "core")


def gelu_grad(preact, upstream):
    pullback = jax.vjp(jax.nn.gelu, preact)[1]
    return pullback(upstream)[0]


def softmax_back(probabilities, upstream, over_axis):
    inner = jnp.sum(probabilities * upstream, axis=over_axis, keepdims=True)
    return probabilities * (upstream - inner)


def local(tokens, slot_params, w_up, w_down, cotangent):
    feat_quarter = tokens.shape[1]
    images = tokens.shape[0] // SEQ
    columns = slot_params.shape[1]
    experts = columns // SLOTS
    up_matrix = w_up[0]
    down_matrix = w_down[0]
    inputs = tokens.reshape(images, SEQ, feat_quarter)
    upstream = cotangent.reshape(images, SEQ, feat_quarter)
    partial_logits = jnp.einsum(
        "imf,fc->imc", inputs, slot_params, preferred_element_type=jnp.float32
    )
    logits = lax.psum(partial_logits, HALF)
    dispatch = jax.nn.softmax(logits, axis=1)
    combine = jax.nn.softmax(logits, axis=2)
    dispatch_bf = dispatch.astype(jnp.bfloat16).reshape(images, SEQ, experts, SLOTS)
    combine_bf = combine.astype(jnp.bfloat16).reshape(images, SEQ, experts, SLOTS)
    slot_in = jnp.einsum(
        "imes,imf->sife", dispatch_bf, inputs, preferred_element_type=jnp.float32
    ).astype(jnp.bfloat16)
    received = lax.all_to_all(slot_in, EXPERT, split_axis=3, concat_axis=3, tiled=True)
    up_slice = up_matrix
    preact = jnp.einsum(
        "sifr,fk->sirk",
        lax.all_gather(received, HALF, axis=2, tiled=True),
        up_slice,
        preferred_element_type=jnp.float32,
    )
    hidden = jax.nn.gelu(preact).astype(jnp.bfloat16)
    down_slice = down_matrix
    summed = lax.psum(
        jnp.einsum("kf,sirk->fsir", down_slice, hidden, preferred_element_type=jnp.float32).astype(
            jnp.bfloat16
        ),
        HALF,
    ).astype(jnp.float32)
    slot_out = lax.dynamic_slice_in_dim(
        summed, lax.axis_index(HALF) * feat_quarter, feat_quarter, 0
    )
    returned = lax.all_to_all(
        slot_out.astype(jnp.bfloat16), EXPERT, split_axis=3, concat_axis=3, tiled=True
    )
    mixed = jnp.einsum(
        "imes,fsie->imf", combine_bf, returned, preferred_element_type=jnp.float32
    ).astype(jnp.bfloat16)
    grad_slot_out = jnp.einsum(
        "imes,imf->sife", combine_bf, upstream, preferred_element_type=jnp.float32
    ).astype(jnp.bfloat16)
    combine_part = jnp.einsum(
        "imf,fsie->imes", upstream, returned, preferred_element_type=jnp.float32
    ).reshape(images, SEQ, columns)
    grad_combine = lax.psum(combine_part.astype(jnp.bfloat16), HALF).astype(jnp.float32)
    grad_received = lax.all_to_all(grad_slot_out, EXPERT, split_axis=3, concat_axis=3, tiled=True)
    down_slice = down_matrix
    grad_hidden = jnp.einsum(
        "sifr,kf->sirk",
        lax.all_gather(grad_received, HALF, axis=2, tiled=True),
        down_slice,
        preferred_element_type=jnp.float32,
    )
    grad_preact = gelu_grad(preact, grad_hidden).astype(jnp.bfloat16)
    up_slice = up_matrix
    summed_grad = lax.psum(
        jnp.einsum(
            "fk,sirk->fsir", up_slice, grad_preact, preferred_element_type=jnp.float32
        ).astype(jnp.bfloat16),
        HALF,
    ).astype(jnp.float32)
    grad_slot_in = lax.dynamic_slice_in_dim(
        summed_grad, lax.axis_index(HALF) * feat_quarter, feat_quarter, 0
    )
    grad_returned = lax.all_to_all(
        grad_slot_in.astype(jnp.bfloat16), EXPERT, split_axis=3, concat_axis=3, tiled=True
    )
    dispatch_part = jnp.einsum(
        "imf,fsie->imes", inputs, grad_returned, preferred_element_type=jnp.float32
    ).reshape(images, SEQ, columns)
    grad_dispatch = lax.psum(dispatch_part.astype(jnp.bfloat16), HALF).astype(jnp.float32)
    grad_logits = softmax_back(combine, grad_combine, 2) + softmax_back(dispatch, grad_dispatch, 1)
    grad_logit_bf = grad_logits.astype(jnp.bfloat16)
    token_term = jnp.einsum(
        "imes,fsie->imf", dispatch_bf, grad_returned, preferred_element_type=jnp.float32
    )
    logit_term = jnp.einsum(
        "imc,fc->imf", grad_logit_bf, slot_params, preferred_element_type=jnp.float32
    )
    grad_tokens = (token_term + logit_term).astype(jnp.bfloat16).reshape(images * SEQ, feat_quarter)
    params_part = jnp.einsum(
        "imf,imc->fc", inputs, grad_logit_bf, preferred_element_type=jnp.float32
    )
    grad_params = lax.psum(lax.psum(lax.psum(params_part, "z"), "y"), "x_lo")
    return (mixed.reshape(images * SEQ, feat_quarter), grad_tokens, grad_params)


def solution(mesh):
    mesh = jax.sharding.Mesh(mesh.devices.reshape(4, 2, 16, 2, 2), EXPERT + HALF)
    in_specs = (
        P(EXPERT, HALF),
        P(HALF, None),
        P(EXPERT, None, HALF),
        P(EXPERT, HALF, None),
        P(EXPERT, HALF),
    )
    out_specs = (P(EXPERT, HALF), P(EXPERT, HALF), P(HALF, None))
    return jax.shard_map(local, mesh=mesh, in_specs=in_specs, out_specs=out_specs, check_vma=False)
```

```python
import functools

import jax
import jax.numpy as jnp
from jax import lax
from jax.experimental import pallas as pl
from jax.experimental.pallas import tpu as pltpu
from jax.sharding import PartitionSpec as P

SEQ = 196
BF16 = jnp.bfloat16
F32 = jnp.float32
EXPERT = ("y", "x_lo", "z")
HALF = ("x_hi", "core")
MESH = pl.DeviceIdType.MESH
GELU_C = 0.7978845608
GELU_A = 0.044715


def dot(a, b, ca, cb):
    return lax.dot_general(a, b, (((ca,), (cb,)), ((), ())), preferred_element_type=F32)


def remote(src, dst, send, recv, device):
    return pltpu.make_async_remote_copy(
        src_ref=src,
        dst_ref=dst,
        send_sem=send,
        recv_sem=recv,
        device_id=device,
        device_id_type=MESH,
    )


def drain(ref, sem):
    pltpu.make_async_copy(ref, ref, sem).wait()


def kernel(
    dims,
    tok_ref,
    par_ref,
    up_hbm,
    down_hbm,
    cot_ref,
    mixed_ref,
    gtok_ref,
    gpar_ref,
    up,
    down,
    w_sem,
    par_sc,
    lg_part,
    lg_r1,
    lg_s1,
    lg_r2,
    lg_full,
    lg_send,
    lg_recv,
    disp,
    comb,
    disp_bf,
    comb_bf,
    stage,
    x_a,
    z_a,
    r_a,
    x_b,
    z_b,
    r_b,
    a2a_send,
    a2a_recv,
    rows,
    rows_send,
    rows_recv,
    preact,
    act,
    part,
    part_in,
    pair,
    pair_in,
    rs_send,
    rs_recv,
    slot,
    g_part,
    g_r1,
    g_s1,
    g_r2,
    g_full,
    g_send,
    g_recv,
    p0,
    p1,
    q0,
    q1,
    u0,
    u1,
    v0,
    v1,
    p_send,
    p_recv,
):
    ny, nx, nz, zl = dims
    zh = nz // zl
    nyx = ny * nx
    experts = nyx * nz
    feat = tok_ref.shape[1]
    lanes = feat // 2
    y, x, z = lax.axis_index("y"), lax.axis_index("x_lo"), lax.axis_index("z")
    xh, core = lax.axis_index("x_hi"), lax.axis_index("core")
    yx = y * nx + x
    own = xh * 2 + core
    across = (1 - xh) * 2 + core
    partner = {"core": 1 - core}
    cross = {"x_hi": 1 - xh}

    def yx_peer(step):
        peer = lax.rem(yx + step, nyx)
        return peer, {"y": peer // nx, "x_lo": lax.rem(peer, nx)}

    def z_peer(step):
        peer = lax.rem(z + step, nz)
        return peer, {"z": peer}

    barrier = pltpu.get_barrier_semaphore()

    def greet(device):
        pl.semaphore_signal(barrier, inc=1, device_id=device, device_id_type=MESH)

    greet(partner)
    greet(cross)
    lax.fori_loop(1, nz, lambda d, _: greet(z_peer(d)[1]), None)
    lax.fori_loop(1, nyx, lambda d, _: greet(yx_peer(d)[1]), None)
    load_up = pltpu.make_async_copy(up_hbm, up, w_sem.at[0])
    load_down = pltpu.make_async_copy(down_hbm, down, w_sem.at[1])
    load_up.start()
    load_down.start()

    columns = 2 * experts
    row_id = lax.broadcasted_iota(jnp.int32, (columns, columns), 0)
    col_id = lax.broadcasted_iota(jnp.int32, (columns, columns), 1)
    order = jnp.where(
        col_id == lax.rem(row_id, 2) * experts + row_id // 2, 1.0, 0.0
    ).astype(BF16)
    tok = tok_ref[...]
    par_sc[...] = dot(par_ref[...], order, 1, 0).astype(BF16)
    logits = dot(tok, par_sc[...], 1, 0)
    lg_part[0] = logits[:, :experts]
    lg_part[1] = logits[:, experts:]

    pl.semaphore_wait(barrier, nz + nyx)

    send0 = remote(lg_part.at[1 - core], lg_r1, lg_send.at[0], lg_recv.at[0], partner)
    send0.start()
    send0.wait_recv()
    lg_s1[...] = lg_part[core] + lg_r1[...]
    send1 = remote(lg_s1, lg_r2, lg_send.at[1], lg_recv.at[1], cross)
    send1.start()
    send1.wait_recv()
    lg_full[core] = lg_s1[...] + lg_r2[...]
    send2 = remote(lg_full.at[core], lg_full.at[core], lg_send.at[2], lg_recv.at[2], partner)
    send2.start()
    send2.wait_recv()

    top = jnp.maximum(
        jnp.max(lg_full[0], axis=1, keepdims=True), jnp.max(lg_full[1], axis=1, keepdims=True)
    )
    total = jnp.zeros_like(top)
    for s in range(2):
        e = jnp.exp(lg_full[s] - top)
        comb[s] = e
        total = total + jnp.sum(e, axis=1, keepdims=True)
        w = jnp.exp(lg_full[s] - jnp.max(lg_full[s], axis=0, keepdims=True))
        w = w / jnp.sum(w, axis=0, keepdims=True)
        disp[s] = w
        disp_bf[s] = w.astype(BF16)
    for s in range(2):
        c = comb[s] / total
        comb[s] = c
        comb_bf[s] = c.astype(BF16)

    def interleave(get, out):
        for a in range(2):
            for s in range(2):
                value = get(a, s)
                for k in range(2):
                    stage[pl.ds(a * 4 + s * 2 + k, experts, stride=8), :] = value[
                        :, k * lanes : (k + 1) * lanes
                    ]
        for i in range(nyx):
            block = stage[i * nz * 8 : (i + 1) * nz * 8, :]
            out[i] = block.reshape(nz, 8, lanes).astype(BF16)

    def deinterleave(source, put):
        for i in range(nyx):
            block = source[i].astype(F32)
            stage[i * nz * 8 : (i + 1) * nz * 8, :] = block.reshape(nz * 8, lanes)
        for a in range(2):
            for s in range(2):
                for k in range(2):
                    piece = stage[pl.ds(a * 4 + s * 2 + k, experts, stride=8), :]
                    put(a, s, k, piece.astype(BF16))

    def exchange(src, mid, dst, which):
        s0, r0 = a2a_send.at[which, 0], a2a_recv.at[which, 0]
        s1, r1 = a2a_send.at[which, 1], a2a_recv.at[which, 1]

        def z_send(step, _):
            peer, device = z_peer(step)
            remote(src.at[:, peer], mid.at[z], s0, r0, device).start()

        lax.fori_loop(1, nz, z_send, None)
        pltpu.make_async_copy(src.at[:, z], mid.at[z], r0).start()
        drain(mid, r0)

        def yx_send(step, _):
            peer, device = yx_peer(step)
            remote(mid.at[:, peer], dst.at[yx], s1, r1, device).start()

        lax.fori_loop(1, nyx, yx_send, None)
        pltpu.make_async_copy(mid.at[:, yx], dst.at[yx], r1).start()
        drain(dst, r1)

    def slot_rows(a, s):
        if a == 0:
            return dot(disp_bf[s], tok, 0, 0)
        return dot(comb_bf[s], cot_ref[...], 0, 0)

    interleave(slot_rows, x_a)
    exchange(x_a, z_a, r_a, 0)

    def put_rows(a, s, k, piece):
        rows[own, a, s * experts : (s + 1) * experts, k * lanes : (k + 1) * lanes] = piece

    deinterleave(r_a, put_rows)

    to_cross, to_partner, forward = [], [], []
    for a in range(2):
        mine = rows.at[own, a]
        to_cross.append(remote(mine, mine, rows_send.at[0, a], rows_recv.at[0, a], cross))
        to_partner.append(remote(mine, mine, rows_send.at[1, a], rows_recv.at[1, a], partner))
        to_cross[a].start()
        to_partner[a].start()
    for a in range(2):
        to_cross[a].wait_recv()
        got = rows.at[across, a]
        forward.append(remote(got, got, rows_send.at[2, a], rows_recv.at[2, a], partner))
        forward[a].start()
    for a in range(2):
        to_partner[a].wait_recv()
        forward[a].wait_recv()
    load_up.wait()
    load_down.wait()

    hidden = up.shape[1]
    width = hidden // 4

    def up_step(j, _):
        cols = pl.ds(pl.multiple_of(j * width, width), width)
        acc = jnp.zeros((columns, width), F32)
        for q in range(4):
            acc = acc + dot(rows[q, 0], up[q * feat : (q + 1) * feat, cols], 1, 0)
        preact[:, cols] = acc
        t = jnp.tanh(GELU_C * (acc + GELU_A * acc * acc * acc))
        act[0, :, cols] = (0.5 * acc * (1.0 + t)).astype(BF16)

    lax.fori_loop(0, 4, up_step, None)

    def grad_step(j, _):
        cols = pl.ds(pl.multiple_of(j * width, width), width)
        acc = jnp.zeros((columns, width), F32)
        for q in range(4):
            acc = acc + dot(rows[q, 1], down[cols, q * feat : (q + 1) * feat], 1, 1)
        v = preact[:, cols]
        t = jnp.tanh(GELU_C * (v + GELU_A * v * v * v))
        slope = 0.5 * (1.0 + t) + 0.5 * v * (1.0 - t * t) * (
            GELU_C * (1.0 + 3.0 * GELU_A * v * v)
        )
        act[1, :, cols] = (acc * slope).astype(BF16)

    lax.fori_loop(0, 4, grad_step, None)

    def out_step(j, _):
        cols = pl.ds(pl.multiple_of(j * feat, feat), feat)
        part[j, 0] = dot(act[0], down[:, cols], 1, 0).astype(BF16)
        part[j, 1] = dot(act[1], up[cols, :], 1, 1).astype(BF16)

    lax.fori_loop(0, 4, out_step, None)

    for i in range(2):
        remote(
            part.at[i * 2 + 1 - core], part_in.at[i], rs_send.at[0], rs_recv.at[0], partner
        ).start()
    drain(part_in, rs_recv.at[0])
    for a in range(2):
        pair[a] = (part[across, a].astype(F32) + part_in[1 - xh, a].astype(F32)).astype(BF16)
    send_pair = remote(pair, pair_in, rs_send.at[1], rs_recv.at[1], cross)
    send_pair.start()
    send_pair.wait_recv()

    def slot_result(a, s):
        r = slice(s * experts, (s + 1) * experts)
        kept = part[own, a, r, :].astype(F32) + part_in[xh, a, r, :].astype(F32)
        return kept + pair_in[a, r, :].astype(F32)

    interleave(slot_result, x_b)
    exchange(x_b, z_b, r_b, 1)

    def put_slot(a, s, k, piece):
        slot[a, s, :, k * lanes : (k + 1) * lanes] = piece

    deinterleave(r_b, put_slot)

    for s in range(2):
        g_part[s, 0] = dot(cot_ref[...], slot[0, s], 1, 1).astype(BF16)
        g_part[s, 1] = dot(tok, slot[1, s], 1, 1).astype(BF16)
    send3 = remote(g_part.at[1 - core], g_r1, g_send.at[0], g_recv.at[0], partner)
    send3.start()
    send3.wait_recv()
    g_s1[...] = (g_part[core].astype(F32) + g_r1[...].astype(F32)).astype(BF16)
    send4 = remote(g_s1, g_r2, g_send.at[1], g_recv.at[1], cross)
    send4.start()
    mixed = dot(comb_bf[0], slot[0, 0], 1, 0) + dot(comb_bf[1], slot[0, 1], 1, 0)
    mixed_ref[...] = mixed.astype(BF16)
    token_term = dot(disp_bf[0], slot[1, 0], 1, 0) + dot(disp_bf[1], slot[1, 1], 1, 0)
    send4.wait_recv()
    g_full[core] = (g_s1[...].astype(F32) + g_r2[...].astype(F32)).astype(BF16)
    send5 = remote(g_full.at[core], g_full.at[core], g_send.at[2], g_recv.at[2], partner)
    send5.start()
    send5.wait_recv()

    inner = jnp.zeros_like(top)
    for s in range(2):
        inner = inner + jnp.sum(comb[s] * g_full[s, 0].astype(F32), axis=1, keepdims=True)
    natural = jnp.zeros((tok.shape[0], columns), F32)
    for s in range(2):
        gd = g_full[s, 1].astype(F32)
        through = disp[s] * (gd - jnp.sum(disp[s] * gd, axis=0, keepdims=True))
        gl = (comb[s] * (g_full[s, 0].astype(F32) - inner) + through).astype(BF16)
        half = slice(s * experts, (s + 1) * experts)
        token_term = token_term + dot(gl, par_sc[:, half], 1, 1)
        natural = natural + dot(gl, order[:, half], 1, 1)
    gtok_ref[...] = token_term.astype(BF16)

    gpar = dot(tok, natural.astype(BF16), 0, 0)
    piece = feat // nyx
    for i in range(nyx):
        p0[i] = gpar[i * piece : (i + 1) * piece, :].astype(BF16)

    def scatter(step, _):
        peer, device = yx_peer(step)
        remote(p0.at[peer], p1.at[yx], p_send.at[0], p_recv.at[0], device).start()

    lax.fori_loop(1, nyx, scatter, None)
    pltpu.make_async_copy(p0.at[yx], p1.at[yx], p_recv.at[0]).start()
    drain(p1, p_recv.at[0])

    def summed(ref, count):
        value = ref[0].astype(F32)
        for i in range(1, count):
            value = value + ref[i].astype(F32)
        return value

    low, high = lax.rem(z, zl), z // zl
    q0[...] = summed(p1, nyx).astype(BF16)

    def share_low(step, _):
        peer = high * zl + lax.rem(low + step, zl)
        remote(q0, q1.at[low], p_send.at[1], p_recv.at[1], {"z": peer}).start()

    lax.fori_loop(1, zl, share_low, None)
    pltpu.make_async_copy(q0, q1.at[low], p_recv.at[1]).start()
    drain(q1, p_recv.at[1])
    u0[...] = summed(q1, zl).astype(BF16)

    def share_high(step, _):
        peer = lax.rem(high + step, zh) * zl + low
        remote(u0, u1.at[high], p_send.at[2], p_recv.at[2], {"z": peer}).start()

    lax.fori_loop(1, zh, share_high, None)
    pltpu.make_async_copy(u0, u1.at[high], p_recv.at[2]).start()
    drain(u1, p_recv.at[2])
    v0[...] = summed(u1, zh)

    def gather(step, _):
        _, device = yx_peer(step)
        remote(v0, v1.at[yx], p_send.at[3], p_recv.at[3], device).start()

    lax.fori_loop(1, nyx, gather, None)
    pltpu.make_async_copy(v0, v1.at[yx], p_recv.at[3]).start()
    drain(v1, p_recv.at[3])
    gpar_ref[...] = v1[...]

    for copy in (send0, send1, send2, send3, send4, send5, send_pair):
        copy.wait_send()
    for a in range(2):
        to_cross[a].wait_send()
        to_partner[a].wait_send()
        forward[a].wait_send()
    drain(part_in, rs_send.at[0])
    for which, mid, dst in ((0, z_a, r_a), (1, z_b, r_b)):
        drain(mid.at[pl.ds(0, nz - 1)], a2a_send.at[which, 0])
        if nyx > 1:
            drain(dst.at[pl.ds(0, nyx - 1)], a2a_send.at[which, 1])
    if nyx > 1:
        drain(p1.at[pl.ds(0, nyx - 1)], p_send.at[0])
        drain(v1.at[pl.ds(0, nyx - 1)], p_send.at[3])
    if zl > 1:
        drain(q1.at[pl.ds(0, zl - 1)], p_send.at[1])
    if zh > 1:
        drain(u1.at[pl.ds(0, zh - 1)], p_send.at[2])


def layer(dims, tokens, slot_params, w_up, w_down, cotangent):
    ny, nx, nz, zl = dims
    nyx, zh = ny * nx, nz // zl
    experts = nyx * nz
    seq, feat = tokens.shape
    columns = slot_params.shape[1]
    depth, hidden = w_up.shape[1:]
    lanes = feat // 2
    vmem, dma = pltpu.VMEM, pltpu.SemaphoreType.DMA
    piece = feat // nyx
    tile = (8, lanes)
    scratch = [
        vmem((depth, hidden), BF16),
        vmem((hidden, depth), BF16),
        dma((2,)),
        vmem((feat, columns), BF16),
        vmem((2, seq, experts), F32),
        vmem((seq, experts), F32),
        vmem((seq, experts), F32),
        vmem((seq, experts), F32),
        vmem((2, seq, experts), F32),
        dma((3,)),
        dma((3,)),
        vmem((2, seq, experts), F32),
        vmem((2, seq, experts), F32),
        vmem((2, seq, experts), BF16),
        vmem((2, seq, experts), BF16),
        vmem((8 * experts, lanes), F32),
    ]
    for _ in range(2):
        scratch += [
            vmem((nyx, nz) + tile, BF16),
            vmem((nz, nyx) + tile, BF16),
            vmem((nyx, nz) + tile, BF16),
        ]
    scratch += [
        dma((2, 2)),
        dma((2, 2)),
        vmem((4, 2, columns, feat), BF16),
        dma((3, 2)),
        dma((3, 2)),
        vmem((columns, hidden), F32),
        vmem((2, columns, hidden), BF16),
        vmem((4, 2, columns, feat), BF16),
        vmem((2, 2, columns, feat), BF16),
        vmem((2, columns, feat), BF16),
        vmem((2, columns, feat), BF16),
        dma((2,)),
        dma((2,)),
        vmem((2, 2, experts, feat), BF16),
        vmem((2, 2, seq, experts), BF16),
        vmem((2, seq, experts), BF16),
        vmem((2, seq, experts), BF16),
        vmem((2, seq, experts), BF16),
        vmem((2, 2, seq, experts), BF16),
        dma((3,)),
        dma((3,)),
        vmem((nyx, piece, columns), BF16),
        vmem((nyx, piece, columns), BF16),
        vmem((piece, columns), BF16),
        vmem((zl, piece, columns), BF16),
        vmem((piece, columns), BF16),
        vmem((zh, piece, columns), BF16),
        vmem((piece, columns), F32),
        vmem((nyx, piece, columns), F32),
        dma((4,)),
        dma((4,)),
    ]
    whole = pl.BlockSpec(memory_space=pltpu.VMEM)
    hbm = pl.BlockSpec(memory_space=pl.ANY)
    mixed, grad_tokens, grad_params = pl.pallas_call(
        functools.partial(kernel, dims),
        out_shape=(
            jax.ShapeDtypeStruct((seq, feat), BF16),
            jax.ShapeDtypeStruct((seq, feat), BF16),
            jax.ShapeDtypeStruct((nyx, piece, columns), F32),
        ),
        in_specs=[whole, whole, hbm, hbm, whole],
        out_specs=(whole, whole, whole),
        scratch_shapes=scratch,
        compiler_params=pltpu.CompilerParams(
            collective_id=0, has_side_effects=True, vmem_limit_bytes=48 << 20
        ),
    )(tokens, slot_params, w_up[0], w_down[0], cotangent)
    return mixed, grad_tokens, grad_params.reshape(feat, columns)


def build(mesh, dims):
    in_specs = (
        P(EXPERT, HALF),
        P(HALF, None),
        P(EXPERT, None, HALF),
        P(EXPERT, HALF, None),
        P(EXPERT, HALF),
    )
    out_specs = (P(EXPERT, HALF), P(EXPERT, HALF), P(HALF, None))
    return jax.shard_map(
        functools.partial(layer, dims),
        mesh=mesh,
        in_specs=in_specs,
        out_specs=out_specs,
        check_vma=False,
    )


def solution(mesh):
    return build(
        jax.sharding.Mesh(mesh.devices.reshape(4, 2, 16, 2, 2), EXPERT + HALF), (4, 2, 16, 4)
    )
```

```python
import functools

import jax
import jax.numpy as jnp
from jax import lax
from jax.experimental import pallas as pl
from jax.experimental.pallas import tpu as pltpu
from jax.sharding import PartitionSpec as P

SEQ = 196
BF16 = jnp.bfloat16
F32 = jnp.float32
EXPERT = ("y", "x_lo", "z")
HALF = ("x_hi", "core")
MESH = pl.DeviceIdType.MESH
GELU_C = 0.7978845608
GELU_A = 0.044715


def dot(a, b, ca, cb):
    return lax.dot_general(a, b, (((ca,), (cb,)), ((), ())), preferred_element_type=F32)


def remote(src, dst, send, recv, device):
    return pltpu.make_async_remote_copy(
        src_ref=src,
        dst_ref=dst,
        send_sem=send,
        recv_sem=recv,
        device_id=device,
        device_id_type=MESH,
    )


def drain(ref, sem):
    pltpu.make_async_copy(ref, ref, sem).wait()


def kernel(
    dims,
    tok_hbm,
    par_hbm,
    up_hbm,
    down_hbm,
    cot_hbm,
    mixed_hbm,
    gtok_hbm,
    gpar_hbm,
    tok_ref,
    par_ref,
    cot_ref,
    up,
    down,
    in_sem,
    mixed_ref,
    gtok_ref,
    gpar_ref,
    out_sem,
    par_sc,
    lg_part,
    lg_r1,
    lg_s1,
    lg_r2,
    lg_full,
    lg_send,
    lg_recv,
    disp,
    comb,
    disp_bf,
    comb_bf,
    stage,
    x_buf,
    z_buf,
    r_buf,
    a2a_send,
    a2a_recv,
    rows,
    rows_send,
    rows_recv,
    preact,
    act,
    part,
    part_in,
    pair,
    pair_in,
    rs_send,
    rs_recv,
    slot,
    g_part,
    g_r1,
    g_s1,
    g_r2,
    g_full,
    g_send,
    g_recv,
    p0,
    p1,
    q0,
    q1,
    u0,
    u1,
    v0,
    v1,
    p_send,
    p_recv,
    know_x,
    know_y,
    know_z,
):
    ny, nx, nz, zl = dims
    zh = nz // zl
    nyx = ny * nx
    experts = nyx * nz
    feat = tok_ref.shape[1]
    lanes = feat // 2
    y, x, z = lax.axis_index("y"), lax.axis_index("x_lo"), lax.axis_index("z")
    xh, core = lax.axis_index("x_hi"), lax.axis_index("core")
    yx = y * nx + x
    own = xh * 2 + core
    across = (1 - xh) * 2 + core
    partner = {"core": 1 - core}
    cross = {"x_hi": 1 - xh}
    sent = []

    def start(src, dst, send, recv, device):
        copy = remote(src, dst, send, recv, device)
        copy.start()
        sent.append(copy)
        return copy

    moves = [(dy, dx) for dy in range(ny) for dx in range(nx) if dy + dx]
    moves.sort(key=lambda m: -min(m[0], ny - m[0]) - min(m[1], nx - m[1]))

    def yx_each(action):
        for dy, dx in moves:
            py, px = lax.rem(y + dy, ny), lax.rem(x + dx, nx)
            action(py * nx + px, {"y": py, "x_lo": px})

    def z_peer(step):
        swing = step // 2
        ahead = nz // 2 + jnp.where(lax.rem(step, 2) == 0, -swing, swing)
        peer = lax.rem(z + ahead, nz)
        return peer, {"z": peer}

    loads = []
    for i, (src, dst) in enumerate(
        (
            (tok_hbm, tok_ref),
            (par_hbm, par_ref),
            (cot_hbm, cot_ref),
            (up_hbm, up),
            (down_hbm, down),
        )
    ):
        loads.append(pltpu.make_async_copy(src, dst, in_sem.at[i]))
        loads[i].start()
    barrier = pltpu.get_barrier_semaphore()

    def greet(device):
        pl.semaphore_signal(barrier, inc=1, device_id=device, device_id_type=MESH)

    def z_near(step):
        return [{"z": lax.rem(z + step, nz)}, {"z": lax.rem(z + nz - step, nz)}]

    y_near = [{"y": lax.rem(y + 1, ny)}, {"y": lax.rem(y + ny - 1, ny)}]
    x_near = {"x_lo": lax.rem(x + 1, nx)}
    near = [partner, cross, x_near] + y_near + z_near(1)
    for device in near:
        greet(device)

    def tell(sem, devices):
        for device in devices:
            pl.semaphore_signal(sem, inc=1, device_id=device, device_id_type=MESH)

    columns = 2 * experts
    row_id = lax.broadcasted_iota(jnp.int32, (columns, columns), 0)
    col_id = lax.broadcasted_iota(jnp.int32, (columns, columns), 1)
    order = jnp.where(
        col_id == lax.rem(row_id, 2) * experts + row_id // 2, 1.0, 0.0
    ).astype(BF16)
    loads[0].wait()
    loads[1].wait()
    tok = tok_ref[...]
    par_sc[...] = dot(par_ref[...], order, 1, 0).astype(BF16)
    logits = dot(tok, par_sc[...], 1, 0)
    lg_part[0] = logits[:, :experts]
    lg_part[1] = logits[:, experts:]

    pl.semaphore_wait(barrier, len(near))
    tell(know_z.at[0], z_near(1))
    tell(know_y, y_near)

    start(lg_part.at[1 - core], lg_r1, lg_send.at[0], lg_recv.at[0], partner).wait_recv()
    lg_s1[...] = lg_part[core] + lg_r1[...]
    summed_over = start(lg_s1, lg_r2, lg_send.at[1], lg_recv.at[1], cross)
    pl.semaphore_wait(know_z.at[0], 2)
    tell(know_z.at[1], z_near(2))
    pl.semaphore_wait(know_y, 2)
    tell(know_x, [x_near])
    pl.semaphore_wait(know_z.at[1], 2)
    tell(know_z.at[2], z_near(4))
    summed_over.wait_recv()
    lg_full[core] = lg_s1[...] + lg_r2[...]
    mine = lg_full.at[core]
    start(mine, mine, lg_send.at[2], lg_recv.at[2], partner).wait_recv()

    def interleave(get, out):
        for s in range(2):
            value = get(s)
            for k in range(2):
                stage[pl.ds(s * 2 + k, experts, stride=8), :] = value[
                    :, k * lanes : (k + 1) * lanes
                ]
        for i in range(nyx):
            block = stage[i * nz * 8 : (i + 1) * nz * 8, :].reshape(nz, 8, lanes)
            out[:, i] = block[:, :4, :].astype(BF16)

    def deinterleave(source, put):
        fill = jnp.zeros((nz, 4, lanes), F32)
        for i in range(nyx):
            block = jnp.concatenate([source[i].astype(F32), fill], axis=1)
            stage[i * nz * 8 : (i + 1) * nz * 8, :] = block.reshape(nz * 8, lanes)
        for s in range(2):
            for k in range(2):
                piece = stage[pl.ds(s * 2 + k, experts, stride=8), :]
                put(s, k, piece.astype(BF16))

    def z_start(trip, a):
        src, mid = x_buf.at[trip, a], z_buf.at[trip, a]
        s0, r0 = a2a_send.at[trip, a, 0], a2a_recv.at[trip, a, 0]

        def z_send(step, _):
            peer, device = z_peer(step)
            remote(src.at[peer], mid.at[z], s0, r0, device).start()

        lax.fori_loop(1, nz, z_send, None)
        pltpu.make_async_copy(src.at[z], mid.at[z], r0).start()

    def yx_start(trip, a):
        mid, dst = z_buf.at[trip, a], r_buf.at[trip, a]
        s1, r1 = a2a_send.at[trip, a, 1], a2a_recv.at[trip, a, 1]
        drain(mid, a2a_recv.at[trip, a, 0])

        def yx_send(peer, device):
            remote(mid.at[:, peer], dst.at[yx], s1, r1, device).start()

        yx_each(yx_send)
        pltpu.make_async_copy(mid.at[:, yx], dst.at[yx], r1).start()

    def yx_wait(trip, a):
        drain(r_buf.at[trip, a], a2a_recv.at[trip, a, 1])

    pl.semaphore_wait(know_x, 1)
    pl.semaphore_wait(know_z.at[2], 2)
    for s in range(2):
        w = jnp.exp(lg_full[s] - jnp.max(lg_full[s], axis=0, keepdims=True))
        w = w / jnp.sum(w, axis=0, keepdims=True)
        disp[s] = w
        disp_bf[s] = w.astype(BF16)
    interleave(lambda s: dot(disp_bf[s], tok, 0, 0), x_buf.at[0, 0])
    z_start(0, 0)
    top = jnp.maximum(
        jnp.max(lg_full[0], axis=1, keepdims=True), jnp.max(lg_full[1], axis=1, keepdims=True)
    )
    total = jnp.zeros_like(top)
    for s in range(2):
        e = jnp.exp(lg_full[s] - top)
        comb[s] = e
        total = total + jnp.sum(e, axis=1, keepdims=True)
    for s in range(2):
        c = comb[s] / total
        comb[s] = c
        comb_bf[s] = c.astype(BF16)
    loads[2].wait()
    interleave(lambda s: dot(comb_bf[s], cot_ref[...], 0, 0), x_buf.at[0, 1])
    z_start(0, 1)

    def put_rows(a):
        def put(s, k, piece):
            rows[own, a, s * experts : (s + 1) * experts, k * lanes : (k + 1) * lanes] = piece

        return put

    def ag_start(a):
        mine = rows.at[own, a]
        start(mine, mine, rows_send.at[0, a], rows_recv.at[0, a], cross)
        start(mine, mine, rows_send.at[1, a], rows_recv.at[1, a], partner)

    def ag_forward(a):
        got = rows.at[across, a]
        drain(got, rows_recv.at[0, a])
        start(got, got, rows_send.at[2, a], rows_recv.at[2, a], partner)

    def ag_wait(a):
        drain(rows.at[0, a], rows_recv.at[1, a])
        drain(rows.at[0, a], rows_recv.at[2, a])

    hidden = up.shape[1]
    width = hidden // 4

    def up_step(j, _):
        cols = pl.ds(pl.multiple_of(j * width, width), width)
        acc = jnp.zeros((columns, width), F32)
        for q in range(4):
            acc = acc + dot(rows[q, 0], up[q * feat : (q + 1) * feat, cols], 1, 0)
        preact[:, cols] = acc
        t = jnp.tanh(GELU_C * (acc + GELU_A * acc * acc * acc))
        act[0, :, cols] = (0.5 * acc * (1.0 + t)).astype(BF16)

    def grad_step(j, _):
        cols = pl.ds(pl.multiple_of(j * width, width), width)
        acc = jnp.zeros((columns, width), F32)
        for q in range(4):
            acc = acc + dot(rows[q, 1], down[cols, q * feat : (q + 1) * feat], 1, 1)
        v = preact[:, cols]
        t = jnp.tanh(GELU_C * (v + GELU_A * v * v * v))
        slope = 0.5 * (1.0 + t) + 0.5 * v * (1.0 - t * t) * (
            GELU_C * (1.0 + 3.0 * GELU_A * v * v)
        )
        act[1, :, cols] = (acc * slope).astype(BF16)

    def quarter(a, j):
        cols = pl.ds(pl.multiple_of(j * feat, feat), feat)
        if a == 0:
            value = dot(act[0], down[:, cols], 1, 0)
        else:
            value = dot(act[1], up[cols, :], 1, 1)
        part[a, j] = value.astype(BF16)

    def rs_start(a):
        for i, half in enumerate((1 - xh, xh)):
            quarter(a, half * 2 + 1 - core)
            start(
                part.at[a, half * 2 + 1 - core],
                part_in.at[a, i],
                rs_send.at[i, a],
                rs_recv.at[i, a],
                partner,
            )
        quarter(a, across)
        quarter(a, own)

    def rs_pair(a):
        drain(part_in.at[a, 0], rs_recv.at[0, a])
        pair[a] = (part[a, across].astype(F32) + part_in[a, 0].astype(F32)).astype(BF16)
        start(pair.at[a], pair_in.at[a], rs_send.at[2, a], rs_recv.at[2, a], cross)

    def rs_finish(a):
        drain(part_in.at[a, 1], rs_recv.at[1, a])
        drain(pair_in.at[a], rs_recv.at[2, a])

        def result(s):
            r = slice(s * experts, (s + 1) * experts)
            kept = part[a, own, r, :].astype(F32) + part_in[a, 1, r, :].astype(F32)
            return kept + pair_in[a, r, :].astype(F32)

        interleave(result, x_buf.at[1, a])
        z_start(1, a)

    yx_start(0, 0)
    yx_wait(0, 0)
    deinterleave(r_buf.at[0, 0], put_rows(0))
    ag_start(0)
    yx_start(0, 1)
    ag_forward(0)
    yx_wait(0, 1)
    deinterleave(r_buf.at[0, 1], put_rows(1))
    ag_start(1)
    ag_wait(0)
    loads[3].wait()
    lax.fori_loop(0, 4, up_step, None)
    loads[4].wait()
    ag_forward(1)
    rs_start(0)
    rs_pair(0)
    ag_wait(1)
    lax.fori_loop(0, 4, grad_step, None)
    rs_start(1)
    rs_pair(1)
    rs_finish(0)
    rs_finish(1)

    def put_slot(a):
        def put(s, k, piece):
            slot[a, s, :, k * lanes : (k + 1) * lanes] = piece

        return put

    def g_start(kind):
        start(g_part.at[kind, 1 - core], g_r1.at[kind], g_send.at[0, kind], g_recv.at[0, kind], partner)

    def g_pair(kind):
        drain(g_r1.at[kind], g_recv.at[0, kind])
        g_s1[kind] = (g_part[kind, core].astype(F32) + g_r1[kind].astype(F32)).astype(BF16)
        start(g_s1.at[kind], g_r2.at[kind], g_send.at[1, kind], g_recv.at[1, kind], cross)

    def g_share(kind):
        drain(g_r2.at[kind], g_recv.at[1, kind])
        g_full[kind, core] = (g_s1[kind].astype(F32) + g_r2[kind].astype(F32)).astype(BF16)
        mine = g_full.at[kind, core]
        start(mine, mine, g_send.at[2, kind], g_recv.at[2, kind], partner)

    def g_wait(kind):
        drain(g_full.at[kind, 0], g_recv.at[2, kind])

    yx_start(1, 0)
    yx_wait(1, 0)
    deinterleave(r_buf.at[1, 0], put_slot(0))
    for s in range(2):
        g_part[0, s] = dot(cot_ref[...], slot[0, s], 1, 1).astype(BF16)
    g_start(0)
    yx_start(1, 1)
    g_pair(0)
    mixed = dot(comb_bf[0], slot[0, 0], 1, 0) + dot(comb_bf[1], slot[0, 1], 1, 0)
    mixed_ref[...] = mixed.astype(BF16)
    store_mixed = pltpu.make_async_copy(mixed_ref, mixed_hbm, out_sem.at[0])
    store_mixed.start()
    yx_wait(1, 1)
    deinterleave(r_buf.at[1, 1], put_slot(1))
    for s in range(2):
        g_part[1, s] = dot(tok, slot[1, s], 1, 1).astype(BF16)
    g_start(1)
    g_share(0)
    g_pair(1)
    token_term = dot(disp_bf[0], slot[1, 0], 1, 0) + dot(disp_bf[1], slot[1, 1], 1, 0)
    g_wait(0)
    inner = jnp.zeros_like(top)
    for s in range(2):
        inner = inner + jnp.sum(comb[s] * g_full[0, s].astype(F32), axis=1, keepdims=True)
    for s in range(2):
        comb[s] = comb[s] * (g_full[0, s].astype(F32) - inner)
    g_share(1)
    g_wait(1)

    natural = jnp.zeros((tok.shape[0], columns), F32)
    grads = []
    for s in range(2):
        gd = g_full[1, s].astype(F32)
        through = disp[s] * (gd - jnp.sum(disp[s] * gd, axis=0, keepdims=True))
        grads.append((comb[s] + through).astype(BF16))
        half = slice(s * experts, (s + 1) * experts)
        natural = natural + dot(grads[s], order[:, half], 1, 1)

    gpar = dot(tok, natural.astype(BF16), 0, 0)
    piece = feat // nyx
    for i in range(nyx):
        p0[i] = gpar[i * piece : (i + 1) * piece, :].astype(BF16)

    def scatter(peer, device):
        remote(p0.at[peer], p1.at[yx], p_send.at[0], p_recv.at[0], device).start()

    yx_each(scatter)
    pltpu.make_async_copy(p0.at[yx], p1.at[yx], p_recv.at[0]).start()
    for s in range(2):
        half = slice(s * experts, (s + 1) * experts)
        token_term = token_term + dot(grads[s], par_sc[:, half], 1, 1)
    gtok_ref[...] = token_term.astype(BF16)
    store_gtok = pltpu.make_async_copy(gtok_ref, gtok_hbm, out_sem.at[1])
    store_gtok.start()
    drain(p1, p_recv.at[0])

    def summed(ref, count):
        value = ref[0].astype(F32)
        for i in range(1, count):
            value = value + ref[i].astype(F32)
        return value

    low, high = lax.rem(z, zl), z // zl
    q0[...] = summed(p1, nyx).astype(BF16)

    def share_low(step, _):
        peer = high * zl + lax.rem(low + step, zl)
        remote(q0, q1.at[low], p_send.at[1], p_recv.at[1], {"z": peer}).start()

    lax.fori_loop(1, zl, share_low, None)
    pltpu.make_async_copy(q0, q1.at[low], p_recv.at[1]).start()
    drain(q1, p_recv.at[1])
    u0[...] = summed(q1, zl).astype(BF16)

    def share_high(step, _):
        ahead = jnp.where(step == 1, zh // 2, jnp.where(step <= zh // 2, step - 1, step))
        peer = lax.rem(high + ahead, zh) * zl + low
        remote(u0, u1.at[high], p_send.at[2], p_recv.at[2], {"z": peer}).start()

    lax.fori_loop(1, zh, share_high, None)
    pltpu.make_async_copy(u0, u1.at[high], p_recv.at[2]).start()
    drain(u1, p_recv.at[2])
    v0[...] = summed(u1, zh).astype(BF16)

    def gather(_, device):
        remote(v0, v1.at[yx], p_send.at[3], p_recv.at[3], device).start()

    yx_each(gather)
    pltpu.make_async_copy(v0, v1.at[yx], p_recv.at[3]).start()
    drain(v1, p_recv.at[3])
    gpar_ref[...] = v1[...].astype(F32)
    store_gpar = pltpu.make_async_copy(gpar_ref, gpar_hbm, out_sem.at[2])
    store_gpar.start()

    for copy in sent:
        copy.wait_send()
    for trip in range(2):
        for a in range(2):
            drain(z_buf.at[trip, a, pl.ds(0, nz - 1)], a2a_send.at[trip, a, 0])
            if nyx > 1:
                drain(r_buf.at[trip, a, pl.ds(0, nyx - 1)], a2a_send.at[trip, a, 1])
    if nyx > 1:
        drain(p1.at[pl.ds(0, nyx - 1)], p_send.at[0])
        drain(v1.at[pl.ds(0, nyx - 1)], p_send.at[3])
    if zl > 1:
        drain(q1.at[pl.ds(0, zl - 1)], p_send.at[1])
    if zh > 1:
        drain(u1.at[pl.ds(0, zh - 1)], p_send.at[2])
    store_mixed.wait()
    store_gtok.wait()
    store_gpar.wait()


def publish(*refs):
    sources, targets, held, sem = refs[:3], refs[3:6], refs[6:9], refs[9]
    fetch = [pltpu.make_async_copy(sources[i], held[i], sem.at[0, i]) for i in range(3)]
    store = [pltpu.make_async_copy(held[i], targets[i], sem.at[1, i]) for i in range(3)]
    for copy in fetch:
        copy.start()
    for i in range(3):
        fetch[i].wait()
        store[i].start()
    for copy in store:
        copy.wait()


def layer(dims, tokens, slot_params, w_up, w_down, cotangent):
    ny, nx, nz, zl = dims
    nyx, zh = ny * nx, nz // zl
    experts = nyx * nz
    seq, feat = tokens.shape
    columns = slot_params.shape[1]
    depth, hidden = w_up.shape[1:]
    lanes = feat // 2
    vmem, dma = pltpu.VMEM, pltpu.SemaphoreType.DMA
    piece = feat // nyx
    scratch = [
        vmem((seq, feat), BF16),
        vmem((feat, columns), BF16),
        vmem((seq, feat), BF16),
        vmem((depth, hidden), BF16),
        vmem((hidden, depth), BF16),
        dma((5,)),
        vmem((seq, feat), BF16),
        vmem((seq, feat), BF16),
        vmem((nyx, piece, columns), F32),
        dma((3,)),
        vmem((feat, columns), BF16),
        vmem((2, seq, experts), F32),
        vmem((seq, experts), F32),
        vmem((seq, experts), F32),
        vmem((seq, experts), F32),
        vmem((2, seq, experts), F32),
        dma((3,)),
        dma((3,)),
        vmem((2, seq, experts), F32),
        vmem((2, seq, experts), F32),
        vmem((2, seq, experts), BF16),
        vmem((2, seq, experts), BF16),
        vmem((8 * experts, lanes), F32),
        vmem((2, 2, nz, nyx, 4, lanes), BF16),
        vmem((2, 2, nz, nyx, 4, lanes), BF16),
        vmem((2, 2, nyx, nz, 4, lanes), BF16),
        dma((2, 2, 2)),
        dma((2, 2, 2)),
        vmem((4, 2, columns, feat), BF16),
        dma((3, 2)),
        dma((3, 2)),
        vmem((columns, hidden), F32),
        vmem((2, columns, hidden), BF16),
        vmem((2, 4, columns, feat), BF16),
        vmem((2, 2, columns, feat), BF16),
        vmem((2, columns, feat), BF16),
        vmem((2, columns, feat), BF16),
        dma((3, 2)),
        dma((3, 2)),
        vmem((2, 2, experts, feat), BF16),
        vmem((2, 2, seq, experts), BF16),
        vmem((2, seq, experts), BF16),
        vmem((2, seq, experts), BF16),
        vmem((2, seq, experts), BF16),
        vmem((2, 2, seq, experts), BF16),
        dma((3, 2)),
        dma((3, 2)),
        vmem((nyx, piece, columns), BF16),
        vmem((nyx, piece, columns), BF16),
        vmem((piece, columns), BF16),
        vmem((zl, piece, columns), BF16),
        vmem((piece, columns), BF16),
        vmem((zh, piece, columns), BF16),
        vmem((piece, columns), BF16),
        vmem((nyx, piece, columns), BF16),
        dma((4,)),
        dma((4,)),
        pltpu.SemaphoreType.REGULAR,
        pltpu.SemaphoreType.REGULAR,
        pltpu.SemaphoreType.REGULAR((3,)),
    ]
    hbm = pl.BlockSpec(memory_space=pltpu.HBM)
    results = pl.pallas_call(
        functools.partial(kernel, dims),
        out_shape=(
            jax.ShapeDtypeStruct((seq, feat), BF16),
            jax.ShapeDtypeStruct((seq, feat), BF16),
            jax.ShapeDtypeStruct((nyx, piece, columns), F32),
        ),
        in_specs=[hbm] * 5,
        out_specs=(hbm, hbm, hbm),
        scratch_shapes=scratch,
        compiler_params=pltpu.CompilerParams(
            collective_id=0, has_side_effects=True, vmem_limit_bytes=67043328
        ),
    )(tokens, slot_params, w_up[0], w_down[0], cotangent)
    mixed, grad_tokens, grad_params = pl.pallas_call(
        publish,
        out_shape=tuple(jax.ShapeDtypeStruct(r.shape, r.dtype) for r in results),
        in_specs=[hbm] * 3,
        out_specs=(hbm, hbm, hbm),
        scratch_shapes=[vmem(r.shape, r.dtype) for r in results] + [dma((2, 3))],
        compiler_params=pltpu.CompilerParams(vmem_limit_bytes=67043328),
    )(*results)
    return mixed, grad_tokens, grad_params.reshape(feat, columns)


def build(mesh, dims):
    in_specs = (
        P(EXPERT, HALF),
        P(HALF, None),
        P(EXPERT, None, HALF),
        P(EXPERT, HALF, None),
        P(EXPERT, HALF),
    )
    out_specs = (P(EXPERT, HALF), P(EXPERT, HALF), P(HALF, None))
    return jax.shard_map(
        functools.partial(layer, dims),
        mesh=mesh,
        in_specs=in_specs,
        out_specs=out_specs,
        check_vma=False,
    )


def solution(mesh):
    return build(
        jax.sharding.Mesh(mesh.devices.reshape(4, 2, 16, 2, 2), EXPERT + HALF), (4, 2, 16, 4)
    )
```

```python
import functools

import jax
import jax.numpy as jnp
from jax import lax
from jax.experimental import pallas as pl
from jax.experimental.pallas import tpu as pltpu
from jax.sharding import PartitionSpec as P

SEQ = 196
BF16 = jnp.bfloat16
F32 = jnp.float32
EXPERT = ("y", "x_lo", "z")
HALF = ("x_hi", "core")
MESH = pl.DeviceIdType.MESH
GELU_C = 0.7978845608
GELU_A = 0.044715


def dot(a, b, ca, cb):
    return lax.dot_general(a, b, (((ca,), (cb,)), ((), ())), preferred_element_type=F32)


def remote(src, dst, send, recv, device):
    return pltpu.make_async_remote_copy(
        src_ref=src,
        dst_ref=dst,
        send_sem=send,
        recv_sem=recv,
        device_id=device,
        device_id_type=MESH,
    )


def drain(ref, sem):
    pltpu.make_async_copy(ref, ref, sem).wait()


def kernel(
    dims,
    tok_hbm,
    par_hbm,
    up_hbm,
    down_hbm,
    cot_hbm,
    mixed_hbm,
    gtok_hbm,
    gpar_hbm,
    tok_ref,
    par_ref,
    cot_ref,
    up,
    down,
    in_sem,
    mixed_ref,
    gtok_ref,
    gpar_ref,
    out_sem,
    par_sc,
    lg_part,
    lg_r1,
    lg_s1,
    lg_r2,
    lg_full,
    lg_send,
    lg_recv,
    disp,
    comb,
    disp_bf,
    comb_bf,
    stage,
    x_buf,
    z_buf,
    r_buf,
    back_buf,
    w_buf,
    a2a_send,
    a2a_recv,
    rows,
    rows_send,
    rows_recv,
    preact,
    act,
    part,
    part_in,
    rs_send,
    rs_recv,
    slot,
    g_part,
    g_r1,
    g_s1,
    g_r2,
    g_full,
    g_send,
    g_recv,
    p0,
    p1,
    q0,
    q1,
    u0,
    u1,
    v0,
    v1,
    p_send,
    p_recv,
    know_x,
    know_y,
    know_z,
):
    ny, nx, nz, zl = dims
    zh = nz // zl
    nyx = ny * nx
    experts = nyx * nz
    feat = tok_ref.shape[1]
    lanes = feat // 2
    y, x, z = lax.axis_index("y"), lax.axis_index("x_lo"), lax.axis_index("z")
    xh, core = lax.axis_index("x_hi"), lax.axis_index("core")
    yx = y * nx + x
    own = xh * 2 + core
    across = (1 - xh) * 2 + core
    partner = {"core": 1 - core}
    cross = {"x_hi": 1 - xh}
    sent = []

    def start(src, dst, send, recv, device):
        copy = remote(src, dst, send, recv, device)
        copy.start()
        sent.append(copy)
        return copy

    moves = [(dy, dx) for dy in range(ny) for dx in range(nx) if dy + dx]
    moves.sort(key=lambda m: -min(m[0], ny - m[0]) - min(m[1], nx - m[1]))

    def yx_each(action):
        for dy, dx in moves:
            py, px = lax.rem(y + dy, ny), lax.rem(x + dx, nx)
            action(py * nx + px, {"y": py, "x_lo": px})

    def z_peer(step):
        swing = step // 2
        ahead = nz // 2 + jnp.where(lax.rem(step, 2) == 0, -swing, swing)
        peer = lax.rem(z + ahead, nz)
        return peer, {"z": peer}

    loads = []
    for i, (src, dst) in enumerate(
        (
            (tok_hbm, tok_ref),
            (par_hbm, par_ref),
            (cot_hbm, cot_ref),
            (up_hbm, up),
            (down_hbm, down),
        )
    ):
        loads.append(pltpu.make_async_copy(src, dst, in_sem.at[i]))
        loads[i].start()
    barrier = pltpu.get_barrier_semaphore()

    def greet(device):
        pl.semaphore_signal(barrier, inc=1, device_id=device, device_id_type=MESH)

    def z_near(step):
        return [{"z": lax.rem(z + step, nz)}, {"z": lax.rem(z + nz - step, nz)}]

    y_near = [{"y": lax.rem(y + 1, ny)}, {"y": lax.rem(y + ny - 1, ny)}]
    x_near = {"x_lo": lax.rem(x + 1, nx)}
    x_ring = [x_near, cross, {"x_lo": 1 - x, "x_hi": 1 - xh}]
    near = [partner] + x_ring + y_near + z_near(1)
    for device in near:
        greet(device)

    def tell(sem, devices):
        for device in devices:
            pl.semaphore_signal(sem, inc=1, device_id=device, device_id_type=MESH)

    columns = 2 * experts
    row_id = lax.broadcasted_iota(jnp.int32, (columns, columns), 0)
    col_id = lax.broadcasted_iota(jnp.int32, (columns, columns), 1)
    order = jnp.where(
        col_id == lax.rem(row_id, 2) * experts + row_id // 2, 1.0, 0.0
    ).astype(BF16)
    loads[0].wait()
    loads[1].wait()
    tok = tok_ref[...]
    par_sc[...] = dot(par_ref[...], order, 1, 0).astype(BF16)
    logits = dot(tok, par_sc[...], 1, 0)
    lg_part[0] = logits[:, :experts]
    lg_part[1] = logits[:, experts:]

    pl.semaphore_wait(barrier, len(near))
    tell(know_z.at[0], z_near(1))
    tell(know_y, y_near)

    start(lg_part.at[1 - core], lg_r1, lg_send.at[0], lg_recv.at[0], partner).wait_recv()
    lg_s1[...] = lg_part[core] + lg_r1[...]
    summed_over = start(lg_s1, lg_r2, lg_send.at[1], lg_recv.at[1], cross)
    pl.semaphore_wait(know_z.at[0], 2)
    tell(know_z.at[1], z_near(2))
    pl.semaphore_wait(know_y, 2)
    tell(know_x, x_ring)
    pl.semaphore_wait(know_z.at[1], 2)
    tell(know_z.at[2], z_near(4))
    summed_over.wait_recv()
    lg_full[core] = lg_s1[...] + lg_r2[...]
    mine = lg_full.at[core]
    start(mine, mine, lg_send.at[2], lg_recv.at[2], partner).wait_recv()

    def interleave(get, out, by_z):
        for s in range(2):
            value = get(s)
            for k in range(2):
                stage[pl.ds(s * 2 + k, experts, stride=8), :] = value[
                    :, k * lanes : (k + 1) * lanes
                ]
        for i in range(nyx):
            block = stage[i * nz * 8 : (i + 1) * nz * 8, :].reshape(nz, 8, lanes)
            if by_z:
                out[:, i] = block[:, :4, :].astype(BF16)
            else:
                out[i] = block[:, :4, :].astype(BF16)

    def deinterleave(source, put, by_z):
        fill = jnp.zeros((nz, 4, lanes), F32)
        for i in range(nyx):
            block = source[:, i] if by_z else source[i]
            block = jnp.concatenate([block.astype(F32), fill], axis=1)
            stage[i * nz * 8 : (i + 1) * nz * 8, :] = block.reshape(nz * 8, lanes)
        for s in range(2):
            for k in range(2):
                piece = stage[pl.ds(s * 2 + k, experts, stride=8), :]
                put(s, k, piece.astype(BF16))

    def z_start(trip, a):
        src, mid = (x_buf if trip == 0 else w_buf).at[a], z_buf.at[trip, a]
        s0, r0 = a2a_send.at[trip, a, 0], a2a_recv.at[trip, a, 0]

        def z_send(step, _):
            peer, device = z_peer(step)
            remote(src.at[peer], mid.at[z], s0, r0, device).start()

        lax.fori_loop(1, nz, z_send, None)
        pltpu.make_async_copy(src.at[z], mid.at[z], r0).start()

    def z_wait(trip, a):
        drain(z_buf.at[trip, a], a2a_recv.at[trip, a, 0])

    flips = [(dy, fx, fh) for dy in range(ny) for fx in range(nx) for fh in range(2)][1:]
    flips.sort(key=lambda m: -min(m[0], ny - m[0]) - (m[1] if m[1] else 2 * m[2]))

    def wide_start(trip, a, source):
        dst = r_buf.at[trip, a, xh, yx]
        s1, r1 = a2a_send.at[trip, a, 1], a2a_recv.at[trip, a, 1]
        for dy, fx, fh in flips:
            py, px = lax.rem(y + dy, ny), (1 - x if fx else x)
            ph = 1 - xh if fh else xh
            device = {"y": py, "x_lo": px, "x_hi": ph}
            remote(source(ph, py * nx + px), dst, s1, r1, device).start()
        pltpu.make_async_copy(source(xh, yx), dst, r1).start()

    def wide_wait(trip, a):
        drain(r_buf.at[trip, a], a2a_recv.at[trip, a, 1])

    pl.semaphore_wait(know_x, 3)
    pl.semaphore_wait(know_z.at[2], 2)
    for s in range(2):
        w = jnp.exp(lg_full[s] - jnp.max(lg_full[s], axis=0, keepdims=True))
        w = w / jnp.sum(w, axis=0, keepdims=True)
        disp[s] = w
        disp_bf[s] = w.astype(BF16)
    interleave(lambda s: dot(disp_bf[s], tok, 0, 0), x_buf.at[0], True)
    z_start(0, 0)
    top = jnp.maximum(
        jnp.max(lg_full[0], axis=1, keepdims=True), jnp.max(lg_full[1], axis=1, keepdims=True)
    )
    total = jnp.zeros_like(top)
    for s in range(2):
        e = jnp.exp(lg_full[s] - top)
        comb[s] = e
        total = total + jnp.sum(e, axis=1, keepdims=True)
    for s in range(2):
        c = comb[s] / total
        comb[s] = c
        comb_bf[s] = c.astype(BF16)
    loads[2].wait()
    interleave(lambda s: dot(comb_bf[s], cot_ref[...], 0, 0), x_buf.at[1], True)
    z_start(0, 1)

    def put_rows(a, h):
        def put(s, k, piece):
            rows[a, core, h, s * experts : (s + 1) * experts, k * lanes : (k + 1) * lanes] = piece

        return put

    def share(a):
        wide_wait(0, a)
        for h in range(2):
            deinterleave(r_buf.at[0, a, h], put_rows(a, h), False)
        mine = rows.at[a, core]
        start(mine, mine, rows_send.at[a], rows_recv.at[a], partner)

    def share_wait(a):
        drain(rows.at[a, 0], rows_recv.at[a])

    hidden = up.shape[1]
    width = hidden // 4

    def features(h, c):
        return pl.ds(pl.multiple_of((h * 2 + c) * feat, feat), feat)

    def up_first(j, _):
        cols = pl.ds(pl.multiple_of(j * width, width), width)
        acc = dot(rows[0, core, 0], up[features(0, core), cols], 1, 0)
        preact[:, cols] = acc + dot(rows[0, core, 1], up[features(1, core), cols], 1, 0)

    def up_step(j, _):
        cols = pl.ds(pl.multiple_of(j * width, width), width)
        acc = preact[:, cols]
        for h in range(2):
            acc = acc + dot(rows[0, 1 - core, h], up[features(h, 1 - core), cols], 1, 0)
        preact[:, cols] = acc
        t = jnp.tanh(GELU_C * (acc + GELU_A * acc * acc * acc))
        act[0, :, cols] = (0.5 * acc * (1.0 + t)).astype(BF16)

    def grad_step(j, _):
        cols = pl.ds(pl.multiple_of(j * width, width), width)
        acc = jnp.zeros((columns, width), F32)
        for q in range(4):
            acc = acc + dot(rows[1, q % 2, q // 2], down[cols, q * feat : (q + 1) * feat], 1, 1)
        v = preact[:, cols]
        t = jnp.tanh(GELU_C * (v + GELU_A * v * v * v))
        slope = 0.5 * (1.0 + t) + 0.5 * v * (1.0 - t * t) * (
            GELU_C * (1.0 + 3.0 * GELU_A * v * v)
        )
        act[1, :, cols] = (acc * slope).astype(BF16)

    def quarter(a, j):
        cols = pl.ds(pl.multiple_of(j * feat, feat), feat)
        if a == 0:
            value = dot(act[0], down[:, cols], 1, 0)
        else:
            value = dot(act[1], up[cols, :], 1, 1)
        part[a, j] = value.astype(BF16)

    def rs_start(a):
        for i, half in enumerate((1 - xh, xh)):
            quarter(a, half * 2 + 1 - core)
            start(
                part.at[a, half * 2 + 1 - core],
                part_in.at[a, i],
                rs_send.at[i, a],
                rs_recv.at[i, a],
                partner,
            )
        quarter(a, across)
        quarter(a, own)

    def rs_pair(a):
        for i, half in enumerate((1 - xh, xh)):
            drain(part_in.at[a, i], rs_recv.at[i, a])

            def paired(s, i=i, half=half):
                r = slice(s * experts, (s + 1) * experts)
                mine = part[a, half * 2 + core, r, :].astype(F32)
                return mine + part_in[a, i, r, :].astype(F32)

            interleave(paired, back_buf.at[a, half], False)
        wide_start(1, a, lambda h, peer: back_buf.at[a, h, peer])

    def rs_finish(a):
        wide_wait(1, a)
        for i in range(nyx):
            total = r_buf[1, a, 0, i].astype(F32) + r_buf[1, a, 1, i].astype(F32)
            w_buf[a, :, i] = total.astype(BF16)
        z_start(1, a)

    z_wait(0, 0)
    wide_start(0, 0, lambda h, peer: z_buf.at[0, 0, :, peer])
    z_wait(0, 1)
    wide_start(0, 1, lambda h, peer: z_buf.at[0, 1, :, peer])
    share(0)
    loads[3].wait()
    lax.fori_loop(0, 4, up_first, None, unroll=True)
    share_wait(0)
    lax.fori_loop(0, 4, up_step, None, unroll=True)
    loads[4].wait()
    rs_start(0)
    share(1)
    rs_pair(0)
    share_wait(1)
    lax.fori_loop(0, 4, grad_step, None, unroll=True)
    rs_start(1)
    rs_pair(1)
    rs_finish(0)
    rs_finish(1)

    def put_slot(a):
        def put(s, k, piece):
            slot[a, s, :, k * lanes : (k + 1) * lanes] = piece

        return put

    def g_start(kind):
        start(g_part.at[kind, 1 - core], g_r1.at[kind], g_send.at[0, kind], g_recv.at[0, kind], partner)

    def g_pair(kind):
        drain(g_r1.at[kind], g_recv.at[0, kind])
        g_s1[kind] = (g_part[kind, core].astype(F32) + g_r1[kind].astype(F32)).astype(BF16)
        start(g_s1.at[kind], g_r2.at[kind], g_send.at[1, kind], g_recv.at[1, kind], cross)

    def g_share(kind):
        drain(g_r2.at[kind], g_recv.at[1, kind])
        g_full[kind, core] = (g_s1[kind].astype(F32) + g_r2[kind].astype(F32)).astype(BF16)
        mine = g_full.at[kind, core]
        start(mine, mine, g_send.at[2, kind], g_recv.at[2, kind], partner)

    def g_wait(kind):
        drain(g_full.at[kind, 0], g_recv.at[2, kind])

    z_wait(1, 0)
    deinterleave(z_buf.at[1, 0], put_slot(0), True)
    for s in range(2):
        g_part[0, s] = dot(cot_ref[...], slot[0, s], 1, 1).astype(BF16)
    g_start(0)
    g_pair(0)
    mixed = dot(comb_bf[0], slot[0, 0], 1, 0) + dot(comb_bf[1], slot[0, 1], 1, 0)
    mixed_ref[...] = mixed.astype(BF16)
    store_mixed = pltpu.make_async_copy(mixed_ref, mixed_hbm, out_sem.at[0])
    store_mixed.start()
    z_wait(1, 1)
    deinterleave(z_buf.at[1, 1], put_slot(1), True)
    for s in range(2):
        g_part[1, s] = dot(tok, slot[1, s], 1, 1).astype(BF16)
    g_start(1)
    g_share(0)
    g_pair(1)
    token_term = dot(disp_bf[0], slot[1, 0], 1, 0) + dot(disp_bf[1], slot[1, 1], 1, 0)
    g_wait(0)
    inner = jnp.zeros_like(top)
    for s in range(2):
        inner = inner + jnp.sum(comb[s] * g_full[0, s].astype(F32), axis=1, keepdims=True)
    for s in range(2):
        comb[s] = comb[s] * (g_full[0, s].astype(F32) - inner)
    g_share(1)
    g_wait(1)

    natural = jnp.zeros((tok.shape[0], columns), F32)
    grads = []
    for s in range(2):
        gd = g_full[1, s].astype(F32)
        through = disp[s] * (gd - jnp.sum(disp[s] * gd, axis=0, keepdims=True))
        grads.append((comb[s] + through).astype(BF16))
        half = slice(s * experts, (s + 1) * experts)
        natural = natural + dot(grads[s], order[:, half], 1, 1)

    gpar = dot(tok, natural.astype(BF16), 0, 0)
    piece = feat // nyx
    for i in range(nyx):
        p0[i] = gpar[i * piece : (i + 1) * piece, :].astype(BF16)

    def scatter(peer, device):
        remote(p0.at[peer], p1.at[yx], p_send.at[0], p_recv.at[0], device).start()

    yx_each(scatter)
    pltpu.make_async_copy(p0.at[yx], p1.at[yx], p_recv.at[0]).start()
    for s in range(2):
        half = slice(s * experts, (s + 1) * experts)
        token_term = token_term + dot(grads[s], par_sc[:, half], 1, 1)
    gtok_ref[...] = token_term.astype(BF16)
    store_gtok = pltpu.make_async_copy(gtok_ref, gtok_hbm, out_sem.at[1])
    store_gtok.start()
    drain(p1, p_recv.at[0])

    def summed(ref, count):
        value = ref[0].astype(F32)
        for i in range(1, count):
            value = value + ref[i].astype(F32)
        return value

    low, high = lax.rem(z, zl), z // zl
    q0[...] = summed(p1, nyx).astype(BF16)

    def share_low(step, _):
        peer = high * zl + lax.rem(low + step, zl)
        remote(q0, q1.at[low], p_send.at[1], p_recv.at[1], {"z": peer}).start()

    lax.fori_loop(1, zl, share_low, None)
    pltpu.make_async_copy(q0, q1.at[low], p_recv.at[1]).start()
    drain(q1, p_recv.at[1])
    u0[...] = summed(q1, zl).astype(BF16)

    def share_high(step, _):
        ahead = jnp.where(step == 1, zh // 2, jnp.where(step <= zh // 2, step - 1, step))
        peer = lax.rem(high + ahead, zh) * zl + low
        remote(u0, u1.at[high], p_send.at[2], p_recv.at[2], {"z": peer}).start()

    lax.fori_loop(1, zh, share_high, None)
    pltpu.make_async_copy(u0, u1.at[high], p_recv.at[2]).start()
    drain(u1, p_recv.at[2])
    v0[...] = summed(u1, zh).astype(BF16)

    def gather(_, device):
        remote(v0, v1.at[yx], p_send.at[3], p_recv.at[3], device).start()

    yx_each(gather)
    pltpu.make_async_copy(v0, v1.at[yx], p_recv.at[3]).start()
    drain(v1, p_recv.at[3])
    gpar_ref[...] = v1[...].astype(F32)
    store_gpar = pltpu.make_async_copy(gpar_ref, gpar_hbm, out_sem.at[2])
    store_gpar.start()

    for copy in sent:
        copy.wait_send()
    for trip in range(2):
        for a in range(2):
            drain(z_buf.at[trip, a, pl.ds(0, nz - 1)], a2a_send.at[trip, a, 0])
            drain(r_buf.at[trip, a, 0], a2a_send.at[trip, a, 1])
            drain(r_buf.at[trip, a, 1, pl.ds(0, nyx - 1)], a2a_send.at[trip, a, 1])
    if nyx > 1:
        drain(p1.at[pl.ds(0, nyx - 1)], p_send.at[0])
        drain(v1.at[pl.ds(0, nyx - 1)], p_send.at[3])
    if zl > 1:
        drain(q1.at[pl.ds(0, zl - 1)], p_send.at[1])
    if zh > 1:
        drain(u1.at[pl.ds(0, zh - 1)], p_send.at[2])
    store_mixed.wait()
    store_gtok.wait()
    store_gpar.wait()


def publish(*refs):
    sources, targets, held, sem = refs[:3], refs[3:6], refs[6:9], refs[9]
    fetch = [pltpu.make_async_copy(sources[i], held[i], sem.at[0, i]) for i in range(3)]
    store = [pltpu.make_async_copy(held[i], targets[i], sem.at[1, i]) for i in range(3)]
    for copy in fetch:
        copy.start()
    for i in range(3):
        fetch[i].wait()
        store[i].start()
    for copy in store:
        copy.wait()


def layer(dims, tokens, slot_params, w_up, w_down, cotangent):
    ny, nx, nz, zl = dims
    nyx, zh = ny * nx, nz // zl
    experts = nyx * nz
    seq, feat = tokens.shape
    columns = slot_params.shape[1]
    depth, hidden = w_up.shape[1:]
    lanes = feat // 2
    vmem, dma = pltpu.VMEM, pltpu.SemaphoreType.DMA
    piece = feat // nyx
    scratch = [
        vmem((seq, feat), BF16),
        vmem((feat, columns), BF16),
        vmem((seq, feat), BF16),
        vmem((depth, hidden), BF16),
        vmem((hidden, depth), BF16),
        dma((5,)),
        vmem((seq, feat), BF16),
        vmem((seq, feat), BF16),
        vmem((nyx, piece, columns), F32),
        dma((3,)),
        vmem((feat, columns), BF16),
        vmem((2, seq, experts), F32),
        vmem((seq, experts), F32),
        vmem((seq, experts), F32),
        vmem((seq, experts), F32),
        vmem((2, seq, experts), F32),
        dma((3,)),
        dma((3,)),
        vmem((2, seq, experts), F32),
        vmem((2, seq, experts), F32),
        vmem((2, seq, experts), BF16),
        vmem((2, seq, experts), BF16),
        vmem((8 * experts, lanes), F32),
        vmem((2, nz, nyx, 4, lanes), BF16),
        vmem((2, 2, nz, nyx, 4, lanes), BF16),
        vmem((2, 2, 2, nyx, nz, 4, lanes), BF16),
        vmem((2, 2, nyx, nz, 4, lanes), BF16),
        vmem((2, nz, nyx, 4, lanes), BF16),
        dma((2, 2, 2)),
        dma((2, 2, 2)),
        vmem((2, 2, 2, columns, feat), BF16),
        dma((2,)),
        dma((2,)),
        vmem((columns, hidden), F32),
        vmem((2, columns, hidden), BF16),
        vmem((2, 4, columns, feat), BF16),
        vmem((2, 2, columns, feat), BF16),
        dma((2, 2)),
        dma((2, 2)),
        vmem((2, 2, experts, feat), BF16),
        vmem((2, 2, seq, experts), BF16),
        vmem((2, seq, experts), BF16),
        vmem((2, seq, experts), BF16),
        vmem((2, seq, experts), BF16),
        vmem((2, 2, seq, experts), BF16),
        dma((3, 2)),
        dma((3, 2)),
        vmem((nyx, piece, columns), BF16),
        vmem((nyx, piece, columns), BF16),
        vmem((piece, columns), BF16),
        vmem((zl, piece, columns), BF16),
        vmem((piece, columns), BF16),
        vmem((zh, piece, columns), BF16),
        vmem((piece, columns), BF16),
        vmem((nyx, piece, columns), BF16),
        dma((4,)),
        dma((4,)),
        pltpu.SemaphoreType.REGULAR,
        pltpu.SemaphoreType.REGULAR,
        pltpu.SemaphoreType.REGULAR((3,)),
    ]
    hbm = pl.BlockSpec(memory_space=pltpu.HBM)
    results = pl.pallas_call(
        functools.partial(kernel, dims),
        out_shape=(
            jax.ShapeDtypeStruct((seq, feat), BF16),
            jax.ShapeDtypeStruct((seq, feat), BF16),
            jax.ShapeDtypeStruct((nyx, piece, columns), F32),
        ),
        in_specs=[hbm] * 5,
        out_specs=(hbm, hbm, hbm),
        scratch_shapes=scratch,
        compiler_params=pltpu.CompilerParams(
            collective_id=0, has_side_effects=True, vmem_limit_bytes=67043328
        ),
    )(tokens, slot_params, w_up[0], w_down[0], cotangent)
    mixed, grad_tokens, grad_params = pl.pallas_call(
        publish,
        out_shape=tuple(jax.ShapeDtypeStruct(r.shape, r.dtype) for r in results),
        in_specs=[hbm] * 3,
        out_specs=(hbm, hbm, hbm),
        scratch_shapes=[vmem(r.shape, r.dtype) for r in results] + [dma((2, 3))],
        compiler_params=pltpu.CompilerParams(vmem_limit_bytes=67043328),
    )(*results)
    return mixed, grad_tokens, grad_params.reshape(feat, columns)


def build(mesh, dims):
    in_specs = (
        P(EXPERT, HALF),
        P(HALF, None),
        P(EXPERT, None, HALF),
        P(EXPERT, HALF, None),
        P(EXPERT, HALF),
    )
    out_specs = (P(EXPERT, HALF), P(EXPERT, HALF), P(HALF, None))
    return jax.shard_map(
        functools.partial(layer, dims),
        mesh=mesh,
        in_specs=in_specs,
        out_specs=out_specs,
        check_vma=False,
    )


def solution(mesh):
    return build(
        jax.sharding.Mesh(mesh.devices.reshape(4, 2, 16, 2, 2), EXPERT + HALF), (4, 2, 16, 4)
    )
```

```python
import functools

import jax
import jax.numpy as jnp
from jax import lax
from jax.experimental import pallas as pl
from jax.experimental.pallas import tpu as pltpu
from jax.sharding import PartitionSpec as P

SEQ = 196
BF16 = jnp.bfloat16
F32 = jnp.float32
EXPERT = ("y", "x_lo", "z")
HALF = ("x_hi", "core")
MESH = pl.DeviceIdType.MESH
GELU_C = 0.7978845608
GELU_A = 0.044715


def dot(a, b, ca, cb):
    return lax.dot_general(a, b, (((ca,), (cb,)), ((), ())), preferred_element_type=F32)


def remote(src, dst, send, recv, device):
    return pltpu.make_async_remote_copy(
        src_ref=src,
        dst_ref=dst,
        send_sem=send,
        recv_sem=recv,
        device_id=device,
        device_id_type=MESH,
    )


def drain(ref, sem):
    pltpu.make_async_copy(ref, ref, sem).wait()


def kernel(
    dims,
    tok_hbm,
    par_hbm,
    up_hbm,
    down_hbm,
    cot_hbm,
    mixed_hbm,
    gtok_hbm,
    gpar_hbm,
    tok,
    par_ref,
    cot,
    up,
    down,
    in_sem,
    out_refs,
    out_in,
    mixed_ref,
    gtok_ref,
    gpar_ref,
    out_sem,
    out_send,
    out_recv,
    par_loc,
    par,
    in_send,
    in_recv,
    lg_s1,
    lg_r2,
    lg_full,
    lg_send,
    lg_recv,
    disp,
    comb,
    disp_bf,
    comb_bf,
    stage,
    x_buf,
    z_buf,
    r_buf,
    back_buf,
    w_buf,
    a2a_send,
    a2a_recv,
    rows,
    rows_send,
    rows_recv,
    preact,
    act,
    part,
    part_in,
    rs_send,
    rs_recv,
    slot,
    g_s1,
    g_r2,
    g_send,
    g_recv,
    row_sum,
    row_in,
    p0,
    p1,
    q0,
    u1,
    v0,
    v1,
    p_send,
    p_recv,
    know_x,
    know_y,
    know_z,
):
    ny, nx, nz, zl = dims
    zh = nz // zl
    nyx = ny * nx
    experts = nyx * nz
    seq, feat = tok.shape[1:]
    lanes = feat // 2
    y, x, z = lax.axis_index("y"), lax.axis_index("x_lo"), lax.axis_index("z")
    xh, core = lax.axis_index("x_hi"), lax.axis_index("core")
    yx = y * nx + x
    own = xh * 2 + core
    across = (1 - xh) * 2 + core
    partner = {"core": 1 - core}
    cross = {"x_hi": 1 - xh}
    sent = []

    def start(src, dst, send, recv, device):
        copy = remote(src, dst, send, recv, device)
        copy.start()
        sent.append(copy)
        return copy

    moves = [(dy, dx) for dy in range(ny) for dx in range(nx) if dy + dx]
    moves.sort(key=lambda m: -min(m[0], ny - m[0]) - min(m[1], nx - m[1]))

    def yx_each(action):
        for dy, dx in moves:
            py, px = lax.rem(y + dy, ny), lax.rem(x + dx, nx)
            action(py * nx + px, {"y": py, "x_lo": px})

    def z_peer(step):
        swing = step // 2
        ahead = nz // 2 + jnp.where(lax.rem(step, 2) == 0, -swing, swing)
        peer = lax.rem(z + ahead, nz)
        return peer, {"z": peer}

    loads = []
    for i, (src, dst) in enumerate(
        (
            (tok_hbm, tok.at[core]),
            (par_hbm, par_ref),
            (cot_hbm, cot.at[core]),
            (up_hbm, up),
            (down_hbm, down),
        )
    ):
        loads.append(pltpu.make_async_copy(src, dst, in_sem.at[i]))
        loads[i].start()
    barrier = pltpu.get_barrier_semaphore()

    def greet(device):
        pl.semaphore_signal(barrier, inc=1, device_id=device, device_id_type=MESH)

    def z_near(step):
        return [{"z": lax.rem(z + step, nz)}, {"z": lax.rem(z + nz - step, nz)}]

    y_near = [{"y": lax.rem(y + 1, ny)}, {"y": lax.rem(y + ny - 1, ny)}]
    x_near = {"x_lo": lax.rem(x + 1, nx)}
    x_ring = [x_near, cross, {"x_lo": 1 - x, "x_hi": 1 - xh}]
    near = [partner] + x_ring + y_near + z_near(1) + z_near(2)
    for device in near:
        greet(device)

    def tell(sem, devices):
        for device in devices:
            pl.semaphore_signal(sem, inc=1, device_id=device, device_id_type=MESH)

    columns = 2 * experts
    row_id = lax.broadcasted_iota(jnp.int32, (columns, experts), 0)
    col_id = lax.broadcasted_iota(jnp.int32, (columns, experts), 1)
    pick = [jnp.where(row_id == 2 * col_id + s, 1.0, 0.0).astype(BF16) for s in range(2)]
    loads[1].wait()
    for s in range(2):
        par_loc[s] = dot(par_ref[...], pick[s], 1, 0).astype(BF16)
    par[core] = par_loc[core]
    loads[0].wait()
    lg_s1[...] = dot(tok[core], par[core], 1, 0)

    pl.semaphore_wait(barrier, len(near))
    tell(know_z.at[0], z_near(2))
    tell(know_y, y_near)

    tok_mine, cot_mine = tok.at[core], cot.at[core]
    start(par_loc.at[1 - core], par.at[core], in_send.at[1], in_recv.at[1], partner)
    start(tok_mine, tok_mine, in_send.at[0], in_recv.at[0], partner)
    drain(par.at[0], in_recv.at[1])
    drain(tok.at[0], in_recv.at[0])
    lg_s1[...] = lg_s1[...] + dot(tok[1 - core], par[1 - core], 1, 0)
    summed_over = start(lg_s1, lg_r2, lg_send.at[0], lg_recv.at[0], cross)
    pl.semaphore_wait(know_z.at[0], 2)
    tell(know_z.at[1], z_near(4))
    pl.semaphore_wait(know_y, 2)
    tell(know_x, x_ring)
    loads[2].wait()
    start(cot_mine, cot_mine, in_send.at[2], in_recv.at[2], partner)
    summed_over.wait_recv()
    lg_full[core] = lg_s1[...] + lg_r2[...]
    mine = lg_full.at[core]
    start(mine, mine, lg_send.at[1], lg_recv.at[1], partner)

    def interleave(get, out, by_z):
        for s in range(2):
            value = get(s)
            for k in range(2):
                stage[pl.ds(s * 2 + k, experts, stride=8), :] = value[
                    :, k * lanes : (k + 1) * lanes
                ]
        for i in range(nyx):
            block = stage[i * nz * 8 : (i + 1) * nz * 8, :].reshape(nz, 8, lanes)
            if by_z:
                out[:, i] = block[:, :4, :].astype(BF16)
            else:
                out[i] = block[:, :4, :].astype(BF16)

    def deinterleave(source, put, by_z):
        fill = jnp.zeros((nz, 4, lanes), F32)
        for i in range(nyx):
            block = source[:, i] if by_z else source[i]
            block = jnp.concatenate([block.astype(F32), fill], axis=1)
            stage[i * nz * 8 : (i + 1) * nz * 8, :] = block.reshape(nz * 8, lanes)
        for s in range(2):
            for k in range(2):
                piece = stage[pl.ds(s * 2 + k, experts, stride=8), :]
                put(s, k, piece.astype(BF16))

    def z_start(trip, a):
        src, mid = (x_buf if trip == 0 else w_buf).at[a], z_buf.at[trip, a]
        s0, r0 = a2a_send.at[trip, a, 0], a2a_recv.at[trip, a, 0]

        def z_send(step, _):
            peer, device = z_peer(step)
            remote(src.at[peer], mid.at[z], s0, r0, device).start()

        lax.fori_loop(1, nz, z_send, None)
        pltpu.make_async_copy(src.at[z], mid.at[z], r0).start()

    def z_wait(trip, a):
        drain(z_buf.at[trip, a], a2a_recv.at[trip, a, 0])

    flips = [(dy, fx, fh) for dy in range(ny) for fx in range(nx) for fh in range(2)][1:]
    flips.sort(key=lambda m: -min(m[0], ny - m[0]) - (m[1] if m[1] else 2 * m[2]))

    def wide_start(trip, a, source):
        dst = r_buf.at[trip, a, xh, yx]
        s1, r1 = a2a_send.at[trip, a, 1], a2a_recv.at[trip, a, 1]
        for dy, fx, fh in flips:
            py, px = lax.rem(y + dy, ny), (1 - x if fx else x)
            ph = 1 - xh if fh else xh
            device = {"y": py, "x_lo": px, "x_hi": ph}
            remote(source(ph, py * nx + px), dst, s1, r1, device).start()
        pltpu.make_async_copy(source(xh, yx), dst, r1).start()

    def wide_wait(trip, a):
        drain(r_buf.at[trip, a], a2a_recv.at[trip, a, 1])

    w = jnp.exp(lg_full[core] - jnp.max(lg_full[core], axis=0, keepdims=True))
    w = w / jnp.sum(w, axis=0, keepdims=True)
    disp[...] = w
    disp_bf[...] = w.astype(BF16)
    interleave(lambda i: dot(disp_bf[...], tok[i], 0, 0), x_buf.at[0], True)
    pl.semaphore_wait(know_x, 3)
    pl.semaphore_wait(know_z.at[1], 2)
    z_start(0, 0)
    drain(lg_full.at[0], lg_recv.at[1])
    top = jnp.maximum(
        jnp.max(lg_full[0], axis=1, keepdims=True), jnp.max(lg_full[1], axis=1, keepdims=True)
    )
    total = jnp.sum(jnp.exp(lg_full[0] - top), axis=1, keepdims=True)
    total = total + jnp.sum(jnp.exp(lg_full[1] - top), axis=1, keepdims=True)
    w = jnp.exp(lg_full[core] - top) / total
    comb[...] = w
    comb_bf[...] = w.astype(BF16)
    drain(cot.at[0], in_recv.at[2])
    interleave(lambda i: dot(comb_bf[...], cot[i], 0, 0), x_buf.at[1], True)
    z_start(0, 1)

    def put_rows(a, h):
        def put(i, k, piece):
            rows[a, core, h, i, :, k * lanes : (k + 1) * lanes] = piece

        return put

    def share(a):
        wide_wait(0, a)
        for h in range(2):
            deinterleave(r_buf.at[0, a, h], put_rows(a, h), False)
        mine = rows.at[a, core]
        start(mine, mine, rows_send.at[a], rows_recv.at[a], partner)

    def share_wait(a):
        drain(rows.at[a, 0], rows_recv.at[a])

    hidden = up.shape[1]
    width = hidden // 4

    def up_slot(s):
        def step(j, _):
            cols = pl.ds(pl.multiple_of(j * width, width), width)
            acc = jnp.zeros((experts, width), F32)
            for q in range(4):
                acc = acc + dot(rows[0, s, q // 2, q % 2], up[q * feat : (q + 1) * feat, cols], 1, 0)
            preact[s, :, cols] = acc
            t = jnp.tanh(GELU_C * (acc + GELU_A * acc * acc * acc))
            act[0, s, :, cols] = (0.5 * acc * (1.0 + t)).astype(BF16)

        lax.fori_loop(0, 4, step, None, unroll=True)

    def grad_step(j, _):
        cols = pl.ds(pl.multiple_of(j * width, width), width)
        acc = jnp.zeros((columns, width), F32)
        for q in range(4):
            both = rows[1, :, q // 2, q % 2].reshape(columns, feat)
            acc = acc + dot(both, down[cols, q * feat : (q + 1) * feat], 1, 1)
        v = preact[:, :, cols].reshape(columns, width)
        t = jnp.tanh(GELU_C * (v + GELU_A * v * v * v))
        slope = 0.5 * (1.0 + t) + 0.5 * v * (1.0 - t * t) * (
            GELU_C * (1.0 + 3.0 * GELU_A * v * v)
        )
        act[1, :, :, cols] = (acc * slope).astype(BF16).reshape(2, experts, width)

    def quarter(a, j):
        cols = slice(j * feat, (j + 1) * feat)
        rows_in = act[a].reshape(columns, hidden)
        if a == 0:
            value = dot(rows_in, down[:, cols], 1, 0)
        else:
            value = dot(rows_in, up[cols, :], 1, 1)
        part[a, :, j] = value.astype(BF16).reshape(2, experts, feat)

    def rs_start(a):
        for h in range(2):
            quarter(a, h * 2)
            quarter(a, h * 2 + 1)
            start(
                part.at[a, 1 - core, pl.ds(h * 2, 2)],
                part_in.at[a, pl.ds(h * 2, 2)],
                rs_send.at[a, h],
                rs_recv.at[a, h],
                partner,
            )

    def rs_pair(a):
        for h in range(2):
            drain(part_in.at[a, pl.ds(h * 2, 2)], rs_recv.at[a, h])

            def paired(i, h=h):
                q = h * 2 + i
                return part[a, core, q].astype(F32) + part_in[a, q].astype(F32)

            interleave(paired, back_buf.at[a, h], False)
        wide_start(1, a, lambda h, peer: back_buf.at[a, h, peer])

    def rs_finish(a):
        wide_wait(1, a)
        for i in range(nyx):
            total = r_buf[1, a, 0, i].astype(F32) + r_buf[1, a, 1, i].astype(F32)
            w_buf[a, :, i] = total.astype(BF16)
        z_start(1, a)

    z_wait(0, 0)
    wide_start(0, 0, lambda h, peer: z_buf.at[0, 0, :, peer])
    z_wait(0, 1)
    wide_start(0, 1, lambda h, peer: z_buf.at[0, 1, :, peer])
    share(0)
    loads[3].wait()
    up_slot(core)
    share_wait(0)
    up_slot(1 - core)
    loads[4].wait()
    rs_start(0)
    share(1)
    rs_pair(0)
    share_wait(1)
    lax.fori_loop(0, 4, grad_step, None, unroll=True)
    rs_start(1)
    rs_pair(1)
    rs_finish(0)
    rs_finish(1)

    def put_slot(a):
        def put(i, k, piece):
            slot[a, i, :, k * lanes : (k + 1) * lanes] = piece

        return put

    def g_start(kind, left):
        value = dot(left[0], slot[kind, 0], 1, 1) + dot(left[1], slot[kind, 1], 1, 1)
        g_s1[kind] = value.astype(BF16)
        start(g_s1.at[kind], g_r2.at[kind], g_send.at[kind], g_recv.at[kind], cross)

    def g_get(kind):
        drain(g_r2.at[kind], g_recv.at[kind])
        return g_s1[kind].astype(F32) + g_r2[kind].astype(F32)

    def swap(kind):
        start(
            out_refs.at[kind, 1 - core],
            out_in.at[kind],
            out_send.at[kind],
            out_recv.at[kind],
            partner,
        )

    def swapped(kind):
        drain(out_in.at[kind], out_recv.at[kind])
        return (out_refs[kind, core] + out_in[kind]).astype(BF16)

    z_wait(1, 0)
    deinterleave(z_buf.at[1, 0], put_slot(0), True)
    g_start(0, cot)
    for i in range(2):
        out_refs[0, i] = dot(comb_bf[...], slot[0, i], 1, 0)
    swap(0)
    grad_comb = g_get(0)
    own_sum = jnp.sum(comb[...] * grad_comb, axis=1, keepdims=True)
    row_sum[...] = jnp.broadcast_to(own_sum, row_sum.shape)
    start(row_sum, row_in, in_send.at[3], in_recv.at[3], partner)
    z_wait(1, 1)
    deinterleave(z_buf.at[1, 1], put_slot(1), True)
    g_start(1, tok)
    drain(row_in, in_recv.at[3])
    comb[...] = comb[...] * (grad_comb - (own_sum + row_in[:, :1]))
    for i in range(2):
        out_refs[1, i] = dot(disp_bf[...], slot[1, i], 1, 0)
    mixed_ref[...] = swapped(0)
    store_mixed = pltpu.make_async_copy(mixed_ref, mixed_hbm, out_sem.at[0])
    store_mixed.start()
    gd = g_get(1)

    through = disp[...] * (gd - jnp.sum(disp[...] * gd, axis=0, keepdims=True))
    gl = (comb[...] + through).astype(BF16)

    count = nyx * zl
    piece = feat // count
    for i in range(2):
        p0[:, i] = dot(tok[i], gl, 0, 0).reshape(count, piece, experts).astype(BF16)

    low, high = lax.rem(z, zl), z // zl
    near_moves = [(dy, dx, dz) for dy in range(ny) for dx in range(nx) for dz in range(zl)][1:]
    near_moves.sort(key=lambda m: -min(m[0], ny - m[0]) - m[1] - (2 if m[2] == 2 else m[2] % 2))
    for dy, dx, dz in near_moves:
        py, px, pz = lax.rem(y + dy, ny), lax.rem(x + dx, nx), lax.rem(low + dz, zl)
        remote(
            p0.at[(py * nx + px) * zl + pz],
            p1.at[yx * zl + low],
            p_send.at[0],
            p_recv.at[0],
            {"y": py, "x_lo": px, "z": high * zl + pz},
        ).start()
    pltpu.make_async_copy(p0.at[yx * zl + low], p1.at[yx * zl + low], p_recv.at[0]).start()
    for i in range(2):
        out_refs[1, i] = out_refs[1, i] + dot(gl, par[i], 1, 1)
    swap(1)
    drain(p1, p_recv.at[0])

    value = p1[0].astype(F32)
    for i in range(1, count):
        value = value + p1[i].astype(F32)
    q0[...] = value.astype(BF16)

    def spread(step, _):
        _, device = z_peer(step)
        remote(q0, u1.at[z], p_send.at[1], p_recv.at[1], device).start()

    lax.fori_loop(1, nz, spread, None)
    pltpu.make_async_copy(q0, u1.at[z], p_recv.at[1]).start()
    gtok_ref[...] = swapped(1)
    store_gtok = pltpu.make_async_copy(gtok_ref, gtok_hbm, out_sem.at[1])
    store_gtok.start()
    drain(u1, p_recv.at[1])
    for i in range(zl):
        value = u1[i].astype(F32)
        for j in range(1, zh):
            value = value + u1[j * zl + i].astype(F32)
        v0[:, i] = value.astype(BF16)
    for dy, dx, dc in [(dy, dx, dc) for dy, dx in [*moves, (0, 0)] for dc in range(2)][:-2] + [
        (0, 0, 1)
    ]:
        py, px, pc = lax.rem(y + dy, ny), lax.rem(x + dx, nx), (1 - core if dc else core)
        remote(
            v0.at[pc],
            v1.at[core, yx],
            p_send.at[2],
            p_recv.at[2],
            {"y": py, "x_lo": px, "core": pc},
        ).start()
    pltpu.make_async_copy(v0.at[core], v1.at[core, yx], p_recv.at[2]).start()
    drain(v1, p_recv.at[2])
    value = jnp.zeros((feat, columns), F32)
    for s in range(2):
        half = v1[s].astype(F32).reshape(feat, experts).astype(BF16)
        value = value + dot(half, pick[s], 1, 1)
    gpar_ref[...] = value
    store_gpar = pltpu.make_async_copy(gpar_ref, gpar_hbm, out_sem.at[2])
    store_gpar.start()

    for copy in sent:
        copy.wait_send()
    for trip in range(2):
        for a in range(2):
            drain(z_buf.at[trip, a, pl.ds(0, nz - 1)], a2a_send.at[trip, a, 0])
            drain(r_buf.at[trip, a, 0], a2a_send.at[trip, a, 1])
            drain(r_buf.at[trip, a, 1, pl.ds(0, nyx - 1)], a2a_send.at[trip, a, 1])
    drain(p1.at[pl.ds(0, count - 1)], p_send.at[0])
    drain(u1.at[pl.ds(0, nz - 1)], p_send.at[1])
    drain(v1.at[0], p_send.at[2])
    drain(v1.at[1, pl.ds(0, nyx - 1)], p_send.at[2])
    store_mixed.wait()
    store_gtok.wait()
    store_gpar.wait()


def publish(*refs):
    sources, targets, held, sem = refs[:3], refs[3:6], refs[6:9], refs[9]
    fetch = [pltpu.make_async_copy(sources[i], held[i], sem.at[0, i]) for i in range(3)]
    store = [pltpu.make_async_copy(held[i], targets[i], sem.at[1, i]) for i in range(3)]
    for copy in fetch:
        copy.start()
    for i in range(3):
        fetch[i].wait()
        store[i].start()
    for copy in store:
        copy.wait()


def layer(dims, tokens, slot_params, w_up, w_down, cotangent):
    ny, nx, nz, zl = dims
    nyx, zh = ny * nx, nz // zl
    experts = nyx * nz
    seq, feat = tokens.shape
    columns = slot_params.shape[1]
    depth, hidden = w_up.shape[1:]
    lanes = feat // 2
    vmem, dma = pltpu.VMEM, pltpu.SemaphoreType.DMA
    piece = feat // (nyx * zl)
    scratch = [
        vmem((2, seq, feat), BF16),
        vmem((feat, columns), BF16),
        vmem((2, seq, feat), BF16),
        vmem((depth, hidden), BF16),
        vmem((hidden, depth), BF16),
        dma((5,)),
        vmem((2, 2, seq, feat), F32),
        vmem((2, seq, feat), F32),
        vmem((seq, feat), BF16),
        vmem((seq, feat), BF16),
        vmem((feat, columns), F32),
        dma((3,)),
        dma((2,)),
        dma((2,)),
        vmem((2, feat, experts), BF16),
        vmem((2, feat, experts), BF16),
        dma((4,)),
        dma((4,)),
        vmem((seq, experts), F32),
        vmem((seq, experts), F32),
        vmem((2, seq, experts), F32),
        dma((2,)),
        dma((2,)),
        vmem((seq, experts), F32),
        vmem((seq, experts), F32),
        vmem((seq, experts), BF16),
        vmem((seq, experts), BF16),
        vmem((8 * experts, lanes), F32),
        vmem((2, nz, nyx, 4, lanes), BF16),
        vmem((2, 2, nz, nyx, 4, lanes), BF16),
        vmem((2, 2, 2, nyx, nz, 4, lanes), BF16),
        vmem((2, 2, nyx, nz, 4, lanes), BF16),
        vmem((2, nz, nyx, 4, lanes), BF16),
        dma((2, 2, 2)),
        dma((2, 2, 2)),
        vmem((2, 2, 2, 2, experts, feat), BF16),
        dma((2,)),
        dma((2,)),
        vmem((2, experts, hidden), F32),
        vmem((2, 2, experts, hidden), BF16),
        vmem((2, 2, 4, experts, feat), BF16),
        vmem((2, 4, experts, feat), BF16),
        dma((2, 2)),
        dma((2, 2)),
        vmem((2, 2, experts, feat), BF16),
        vmem((2, seq, experts), BF16),
        vmem((2, seq, experts), BF16),
        dma((2,)),
        dma((2,)),
        vmem((seq, experts), F32),
        vmem((seq, experts), F32),
        vmem((nyx * zl, 2, piece, experts), BF16),
        vmem((nyx * zl, 2, piece, experts), BF16),
        vmem((2, piece, experts), BF16),
        vmem((nz, 2, piece, experts), BF16),
        vmem((2, zl, piece, experts), BF16),
        vmem((2, nyx, zl, piece, experts), BF16),
        dma((3,)),
        dma((3,)),
        pltpu.SemaphoreType.REGULAR,
        pltpu.SemaphoreType.REGULAR,
        pltpu.SemaphoreType.REGULAR((2,)),
    ]
    hbm = pl.BlockSpec(memory_space=pltpu.HBM)
    results = pl.pallas_call(
        functools.partial(kernel, dims),
        out_shape=(
            jax.ShapeDtypeStruct((seq, feat), BF16),
            jax.ShapeDtypeStruct((seq, feat), BF16),
            jax.ShapeDtypeStruct((feat, columns), F32),
        ),
        in_specs=[hbm] * 5,
        out_specs=(hbm, hbm, hbm),
        scratch_shapes=scratch,
        compiler_params=pltpu.CompilerParams(
            collective_id=0, has_side_effects=True, vmem_limit_bytes=67043328
        ),
    )(tokens, slot_params, w_up[0], w_down[0], cotangent)
    mixed, grad_tokens, grad_params = pl.pallas_call(
        publish,
        out_shape=tuple(jax.ShapeDtypeStruct(r.shape, r.dtype) for r in results),
        in_specs=[hbm] * 3,
        out_specs=(hbm, hbm, hbm),
        scratch_shapes=[vmem(r.shape, r.dtype) for r in results] + [dma((2, 3))],
        compiler_params=pltpu.CompilerParams(vmem_limit_bytes=67043328),
    )(*results)
    return mixed, grad_tokens, grad_params


def build(mesh, dims):
    in_specs = (
        P(EXPERT, HALF),
        P(HALF, None),
        P(EXPERT, None, HALF),
        P(EXPERT, HALF, None),
        P(EXPERT, HALF),
    )
    out_specs = (P(EXPERT, HALF), P(EXPERT, HALF), P(HALF, None))
    return jax.shard_map(
        functools.partial(layer, dims),
        mesh=mesh,
        in_specs=in_specs,
        out_specs=out_specs,
        check_vma=False,
    )


def solution(mesh):
    return build(
        jax.sharding.Mesh(mesh.devices.reshape(4, 2, 16, 2, 2), EXPERT + HALF), (4, 2, 16, 4)
    )
```

```python
import functools

import jax
import jax.numpy as jnp
from jax import lax
from jax.experimental import pallas as pl
from jax.experimental.pallas import tpu as pltpu
from jax.sharding import PartitionSpec as P

SEQ = 196
BF16 = jnp.bfloat16
F32 = jnp.float32
EXPERT = ("y", "x_lo", "z")
HALF = ("x_hi", "core")
MESH = pl.DeviceIdType.MESH
GELU_C = 0.7978845608
GELU_A = 0.044715


def dot(a, b, ca, cb):
    return lax.dot_general(a, b, (((ca,), (cb,)), ((), ())), preferred_element_type=F32)


def remote(src, dst, send, recv, device):
    return pltpu.make_async_remote_copy(
        src_ref=src,
        dst_ref=dst,
        send_sem=send,
        recv_sem=recv,
        device_id=device,
        device_id_type=MESH,
    )


def drain(ref, sem):
    pltpu.make_async_copy(ref, ref, sem).wait()


def kernel(
    dims,
    tok_hbm,
    par_hbm,
    up_hbm,
    down_hbm,
    cot_hbm,
    mixed_hbm,
    gtok_hbm,
    gpar_hbm,
    tok,
    par_ref,
    cot,
    up,
    down,
    in_sem,
    out_refs,
    out_in,
    mixed_ref,
    gtok_ref,
    gpar_ref,
    out_sem,
    out_send,
    out_recv,
    par_loc,
    par,
    in_send,
    in_recv,
    lg_s1,
    lg_r2,
    lg_full,
    lg_send,
    lg_recv,
    disp,
    comb,
    disp_bf,
    comb_bf,
    stage,
    x_buf,
    z_buf,
    r_buf,
    back_buf,
    w_buf,
    a2a_send,
    a2a_recv,
    rows,
    rows_send,
    rows_recv,
    preact,
    act,
    part,
    part_in,
    rs_send,
    rs_recv,
    slot,
    g_s1,
    g_r2,
    g_send,
    g_recv,
    row_sum,
    row_in,
    p0,
    p1,
    q0,
    u1,
    v0,
    v1,
    p_send,
    p_recv,
    know_x,
    know_y,
    know_z,
):
    ny, nx, nz, zl = dims
    zh = nz // zl
    nyx = ny * nx
    experts = nyx * nz
    seq, feat = tok.shape[1:]
    lanes = feat // 2
    y, x, z = lax.axis_index("y"), lax.axis_index("x_lo"), lax.axis_index("z")
    xh, core = lax.axis_index("x_hi"), lax.axis_index("core")
    yx = y * nx + x
    own = xh * 2 + core
    across = (1 - xh) * 2 + core
    partner = {"core": 1 - core}
    cross = {"x_hi": 1 - xh}
    sent = []

    def start(src, dst, send, recv, device):
        copy = remote(src, dst, send, recv, device)
        copy.start()
        sent.append(copy)
        return copy

    moves = [(dy, dx) for dy in range(ny) for dx in range(nx) if dy + dx]
    moves.sort(key=lambda m: -min(m[0], ny - m[0]) - min(m[1], nx - m[1]))

    def yx_each(action):
        for dy, dx in moves:
            py, px = lax.rem(y + dy, ny), lax.rem(x + dx, nx)
            action(py * nx + px, {"y": py, "x_lo": px})

    def z_peer(step):
        swing = step // 2
        ahead = nz // 2 + jnp.where(lax.rem(step, 2) == 0, -swing, swing)
        peer = lax.rem(z + ahead, nz)
        return peer, {"z": peer}

    loads = []
    for i, (src, dst) in enumerate(
        (
            (tok_hbm, tok.at[core]),
            (par_hbm, par_ref),
            (cot_hbm, cot.at[core]),
            (up_hbm, up),
            (down_hbm, down),
        )
    ):
        loads.append(pltpu.make_async_copy(src, dst, in_sem.at[i]))
        loads[i].start()
    barrier = pltpu.get_barrier_semaphore()

    def greet(device):
        pl.semaphore_signal(barrier, inc=1, device_id=device, device_id_type=MESH)

    def z_near(step):
        return [{"z": lax.rem(z + step, nz)}, {"z": lax.rem(z + nz - step, nz)}]

    y_near = [{"y": lax.rem(y + 1, ny)}, {"y": lax.rem(y + ny - 1, ny)}]
    x_near = {"x_lo": lax.rem(x + 1, nx)}
    x_ring = [x_near, cross, {"x_lo": 1 - x, "x_hi": 1 - xh}]
    near = [partner] + x_ring + y_near + z_near(1) + z_near(2)
    for device in near:
        greet(device)

    def tell(sem, devices):
        for device in devices:
            pl.semaphore_signal(sem, inc=1, device_id=device, device_id_type=MESH)

    columns = 2 * experts
    row_id = lax.broadcasted_iota(jnp.int32, (columns, experts), 0)
    col_id = lax.broadcasted_iota(jnp.int32, (columns, experts), 1)
    pick = [jnp.where(row_id == 2 * col_id + s, 1.0, 0.0).astype(BF16) for s in range(2)]
    loads[1].wait()
    for s in range(2):
        par_loc[s] = dot(par_ref[...], pick[s], 1, 0).astype(BF16)
    par[core] = par_loc[core]
    loads[0].wait()
    lg_s1[...] = dot(tok[core], par[core], 1, 0)

    pl.semaphore_wait(barrier, len(near))
    tell(know_z.at[0], z_near(2))
    tell(know_y, y_near)

    tok_mine, cot_mine = tok.at[core], cot.at[core]
    start(par_loc.at[1 - core], par.at[core], in_send.at[1], in_recv.at[1], partner)
    start(tok_mine, tok_mine, in_send.at[0], in_recv.at[0], partner)
    drain(par.at[0], in_recv.at[1])
    drain(tok.at[0], in_recv.at[0])
    lg_s1[...] = lg_s1[...] + dot(tok[1 - core], par[1 - core], 1, 0)
    summed_over = start(lg_s1, lg_r2, lg_send.at[0], lg_recv.at[0], cross)
    pl.semaphore_wait(know_z.at[0], 2)
    tell(know_z.at[1], z_near(4))
    pl.semaphore_wait(know_y, 2)
    tell(know_x, x_ring)
    loads[2].wait()
    start(cot_mine, cot_mine, in_send.at[2], in_recv.at[2], partner)
    summed_over.wait_recv()
    lg_full[core] = lg_s1[...] + lg_r2[...]
    mine = lg_full.at[core]
    start(mine, mine, lg_send.at[1], lg_recv.at[1], partner)

    def interleave(get, out, by_z):
        for s in range(2):
            value = get(s)
            for k in range(2):
                stage[pl.ds(s * 2 + k, experts, stride=8), :] = value[
                    :, k * lanes : (k + 1) * lanes
                ]
        for i in range(nyx):
            block = stage[i * nz * 8 : (i + 1) * nz * 8, :].reshape(nz, 8, lanes)
            if by_z:
                out[:, i] = block[:, :4, :].astype(BF16)
            else:
                out[i] = block[:, :4, :].astype(BF16)

    def deinterleave(source, put, by_z):
        fill = jnp.zeros((nz, 4, lanes), F32)
        for i in range(nyx):
            block = source[:, i] if by_z else source[i]
            block = jnp.concatenate([block.astype(F32), fill], axis=1)
            stage[i * nz * 8 : (i + 1) * nz * 8, :] = block.reshape(nz * 8, lanes)
        for s in range(2):
            for k in range(2):
                piece = stage[pl.ds(s * 2 + k, experts, stride=8), :]
                put(s, k, piece.astype(BF16))

    def z_start(trip, a):
        src, mid = (x_buf if trip == 0 else w_buf).at[a], z_buf.at[trip, a]
        s0, r0 = a2a_send.at[trip, a, 0], a2a_recv.at[trip, a, 0]

        def z_send(step, _):
            peer, device = z_peer(step)
            remote(src.at[peer], mid.at[z], s0, r0, device).start()

        lax.fori_loop(1, nz, z_send, None)
        pltpu.make_async_copy(src.at[z], mid.at[z], r0).start()

    def z_wait(trip, a):
        drain(z_buf.at[trip, a], a2a_recv.at[trip, a, 0])

    flips = [(dy, fx, fh) for dy in range(ny) for fx in range(nx) for fh in range(2)][1:]
    flips.sort(key=lambda m: -min(m[0], ny - m[0]) - (m[1] if m[1] else 2 * m[2]))

    def wide_start(trip, a, source, only=None):
        dst = r_buf.at[trip, a, xh, yx]
        s1, r1 = a2a_send.at[trip, a, 1], a2a_recv.at[trip, a, 1]
        for dy, fx, fh in flips:
            if only not in (None, fh):
                continue
            py, px = lax.rem(y + dy, ny), (1 - x if fx else x)
            ph = 1 - xh if fh else xh
            device = {"y": py, "x_lo": px, "x_hi": ph}
            remote(source(ph, py * nx + px), dst, s1, r1, device).start()
        if only != 1:
            pltpu.make_async_copy(source(xh, yx), dst, r1).start()

    def wide_wait(trip, a):
        drain(r_buf.at[trip, a], a2a_recv.at[trip, a, 1])

    w = jnp.exp(lg_full[core] - jnp.max(lg_full[core], axis=0, keepdims=True))
    w = w / jnp.sum(w, axis=0, keepdims=True)
    disp[...] = w
    disp_bf[...] = w.astype(BF16)
    interleave(lambda i: dot(disp_bf[...], tok[i], 0, 0), x_buf.at[0], True)
    pl.semaphore_wait(know_x, 3)
    pl.semaphore_wait(know_z.at[1], 2)
    z_start(0, 0)
    drain(lg_full.at[0], lg_recv.at[1])
    top = jnp.maximum(
        jnp.max(lg_full[0], axis=1, keepdims=True), jnp.max(lg_full[1], axis=1, keepdims=True)
    )
    total = jnp.sum(jnp.exp(lg_full[0] - top), axis=1, keepdims=True)
    total = total + jnp.sum(jnp.exp(lg_full[1] - top), axis=1, keepdims=True)
    w = jnp.exp(lg_full[core] - top) / total
    comb[...] = w
    comb_bf[...] = w.astype(BF16)
    drain(cot.at[0], in_recv.at[2])
    interleave(lambda i: dot(comb_bf[...], cot[i], 0, 0), x_buf.at[1], True)
    z_start(0, 1)

    def put_rows(a, h):
        def put(i, k, piece):
            rows[a, core, h, i, :, k * lanes : (k + 1) * lanes] = piece

        return put

    def share(a):
        wide_wait(0, a)
        for h in range(2):
            deinterleave(r_buf.at[0, a, h], put_rows(a, h), False)
        mine = rows.at[a, core]
        start(mine, mine, rows_send.at[a], rows_recv.at[a], partner)

    def share_wait(a):
        drain(rows.at[a, 0], rows_recv.at[a])

    hidden = up.shape[1]
    width = hidden // 4

    def up_slot(s):
        def step(j, _):
            cols = pl.ds(pl.multiple_of(j * width, width), width)
            acc = jnp.zeros((experts, width), F32)
            for q in range(4):
                acc = acc + dot(rows[0, s, q // 2, q % 2], up[q * feat : (q + 1) * feat, cols], 1, 0)
            preact[s, :, cols] = acc
            t = jnp.tanh(GELU_C * (acc + GELU_A * acc * acc * acc))
            act[0, s, :, cols] = (0.5 * acc * (1.0 + t)).astype(BF16)

        lax.fori_loop(0, 4, step, None, unroll=True)

    def grad_step(j, _):
        cols = pl.ds(pl.multiple_of(j * width, width), width)
        acc = jnp.zeros((columns, width), F32)
        for q in range(4):
            both = rows[1, :, q // 2, q % 2].reshape(columns, feat)
            acc = acc + dot(both, down[cols, q * feat : (q + 1) * feat], 1, 1)
        v = preact[:, :, cols].reshape(columns, width)
        t = jnp.tanh(GELU_C * (v + GELU_A * v * v * v))
        slope = 0.5 * (1.0 + t) + 0.5 * v * (1.0 - t * t) * (
            GELU_C * (1.0 + 3.0 * GELU_A * v * v)
        )
        act[1, :, :, cols] = (acc * slope).astype(BF16).reshape(2, experts, width)

    def quarter(a, j):
        cols = pl.ds(pl.multiple_of(j * feat, feat), feat)
        rows_in = act[a].reshape(columns, hidden)
        if a == 0:
            value = dot(rows_in, down[:, cols], 1, 0)
        else:
            value = dot(rows_in, up[cols, :], 1, 1)
        part[a, :, j] = value.astype(BF16).reshape(2, experts, feat)

    def rs_start(a):
        for h in (1 - xh, xh):
            quarter(a, h * 2)
            quarter(a, h * 2 + 1)
            start(
                part.at[a, 1 - core, pl.ds(h * 2, 2)],
                part_in.at[a, pl.ds(h * 2, 2)],
                rs_send.at[a, h],
                rs_recv.at[a, h],
                partner,
            )

    def rs_pair(a):
        for fh, h in ((1, 1 - xh), (0, xh)):
            drain(part_in.at[a, pl.ds(h * 2, 2)], rs_recv.at[a, h])

            def paired(i, h=h):
                q = h * 2 + i
                return part[a, core, q].astype(F32) + part_in[a, q].astype(F32)

            interleave(paired, back_buf.at[a, h], False)
            wide_start(1, a, lambda h, peer: back_buf.at[a, h, peer], fh)

    def rs_finish(a):
        wide_wait(1, a)
        for i in range(nyx):
            total = r_buf[1, a, 0, i].astype(F32) + r_buf[1, a, 1, i].astype(F32)
            w_buf[a, :, i] = total.astype(BF16)
        z_start(1, a)

    z_wait(0, 0)
    wide_start(0, 0, lambda h, peer: z_buf.at[0, 0, :, peer])
    z_wait(0, 1)
    wide_start(0, 1, lambda h, peer: z_buf.at[0, 1, :, peer])
    share(0)
    loads[3].wait()
    up_slot(core)
    share_wait(0)
    up_slot(1 - core)
    loads[4].wait()
    rs_start(0)
    share(1)
    rs_pair(0)
    share_wait(1)
    lax.fori_loop(0, 4, grad_step, None, unroll=True)
    rs_start(1)
    rs_pair(1)
    rs_finish(0)
    rs_finish(1)

    def put_slot(a):
        def put(i, k, piece):
            slot[a, i, :, k * lanes : (k + 1) * lanes] = piece

        return put

    def g_start(kind, left):
        value = dot(left[0], slot[kind, 0], 1, 1) + dot(left[1], slot[kind, 1], 1, 1)
        g_s1[kind] = value.astype(BF16)
        start(g_s1.at[kind], g_r2.at[kind], g_send.at[kind], g_recv.at[kind], cross)

    def g_get(kind):
        drain(g_r2.at[kind], g_recv.at[kind])
        return g_s1[kind].astype(F32) + g_r2[kind].astype(F32)

    def swap(kind):
        start(
            out_refs.at[kind, 1 - core],
            out_in.at[kind],
            out_send.at[kind],
            out_recv.at[kind],
            partner,
        )

    def swapped(kind):
        drain(out_in.at[kind], out_recv.at[kind])
        return (out_refs[kind, core] + out_in[kind]).astype(BF16)

    z_wait(1, 0)
    deinterleave(z_buf.at[1, 0], put_slot(0), True)
    g_start(0, cot)
    for i in range(2):
        out_refs[0, i] = dot(comb_bf[...], slot[0, i], 1, 0)
    swap(0)
    grad_comb = g_get(0)
    own_sum = jnp.sum(comb[...] * grad_comb, axis=1, keepdims=True)
    row_sum[...] = jnp.broadcast_to(own_sum, row_sum.shape)
    start(row_sum, row_in, in_send.at[3], in_recv.at[3], partner)
    z_wait(1, 1)
    deinterleave(z_buf.at[1, 1], put_slot(1), True)
    g_start(1, tok)
    drain(row_in, in_recv.at[3])
    comb[...] = comb[...] * (grad_comb - (own_sum + row_in[:, :1]))
    for i in range(2):
        out_refs[1, i] = dot(disp_bf[...], slot[1, i], 1, 0)
    mixed_ref[...] = swapped(0)
    store_mixed = pltpu.make_async_copy(mixed_ref, mixed_hbm, out_sem.at[0])
    store_mixed.start()
    gd = g_get(1)

    through = disp[...] * (gd - jnp.sum(disp[...] * gd, axis=0, keepdims=True))
    gl = (comb[...] + through).astype(BF16)

    count = nyx * zl
    piece = feat // count
    for i in range(2):
        p0[:, i] = dot(tok[i], gl, 0, 0).reshape(count, piece, experts).astype(BF16)

    low, high = lax.rem(z, zl), z // zl
    near_moves = [(dy, dx, dz) for dy in range(ny) for dx in range(nx) for dz in range(zl)][1:]
    near_moves.sort(key=lambda m: -min(m[0], ny - m[0]) - m[1] - (2 if m[2] == 2 else m[2] % 2))
    for dy, dx, dz in near_moves:
        py, px, pz = lax.rem(y + dy, ny), lax.rem(x + dx, nx), lax.rem(low + dz, zl)
        remote(
            p0.at[(py * nx + px) * zl + pz],
            p1.at[yx * zl + low],
            p_send.at[0],
            p_recv.at[0],
            {"y": py, "x_lo": px, "z": high * zl + pz},
        ).start()
    pltpu.make_async_copy(p0.at[yx * zl + low], p1.at[yx * zl + low], p_recv.at[0]).start()
    for i in range(2):
        out_refs[1, i] = out_refs[1, i] + dot(gl, par[i], 1, 1)
    swap(1)
    drain(p1, p_recv.at[0])

    value = p1[0].astype(F32)
    for i in range(1, count):
        value = value + p1[i].astype(F32)
    q0[...] = value.astype(BF16)

    def spread(step, _):
        _, device = z_peer(step)
        remote(q0, u1.at[z], p_send.at[1], p_recv.at[1], device).start()

    lax.fori_loop(1, nz, spread, None)
    pltpu.make_async_copy(q0, u1.at[z], p_recv.at[1]).start()
    gtok_ref[...] = swapped(1)
    store_gtok = pltpu.make_async_copy(gtok_ref, gtok_hbm, out_sem.at[1])
    store_gtok.start()
    drain(u1, p_recv.at[1])
    for i in range(zl):
        value = u1[i].astype(F32)
        for j in range(1, zh):
            value = value + u1[j * zl + i].astype(F32)
        v0[:, i] = value.astype(BF16)
    for dy, dx, dc in [(dy, dx, dc) for dy, dx in [*moves, (0, 0)] for dc in range(2)][:-2] + [
        (0, 0, 1)
    ]:
        py, px, pc = lax.rem(y + dy, ny), lax.rem(x + dx, nx), (1 - core if dc else core)
        remote(
            v0.at[pc],
            v1.at[core, yx],
            p_send.at[2],
            p_recv.at[2],
            {"y": py, "x_lo": px, "core": pc},
        ).start()
    pltpu.make_async_copy(v0.at[core], v1.at[core, yx], p_recv.at[2]).start()
    drain(v1, p_recv.at[2])
    value = jnp.zeros((feat, columns), F32)
    for s in range(2):
        half = v1[s].astype(F32).reshape(feat, experts).astype(BF16)
        value = value + dot(half, pick[s], 1, 1)
    gpar_ref[...] = value
    store_gpar = pltpu.make_async_copy(gpar_ref, gpar_hbm, out_sem.at[2])
    store_gpar.start()

    for copy in sent:
        copy.wait_send()
    for trip in range(2):
        for a in range(2):
            drain(z_buf.at[trip, a, pl.ds(0, nz - 1)], a2a_send.at[trip, a, 0])
            drain(r_buf.at[trip, a, 0], a2a_send.at[trip, a, 1])
            drain(r_buf.at[trip, a, 1, pl.ds(0, nyx - 1)], a2a_send.at[trip, a, 1])
    drain(p1.at[pl.ds(0, count - 1)], p_send.at[0])
    drain(u1.at[pl.ds(0, nz - 1)], p_send.at[1])
    drain(v1.at[0], p_send.at[2])
    drain(v1.at[1, pl.ds(0, nyx - 1)], p_send.at[2])
    store_mixed.wait()
    store_gtok.wait()
    store_gpar.wait()


def publish(*refs):
    sources, targets, held, sem = refs[:3], refs[3:6], refs[6:9], refs[9]
    fetch = [pltpu.make_async_copy(sources[i], held[i], sem.at[0, i]) for i in range(3)]
    store = [pltpu.make_async_copy(held[i], targets[i], sem.at[1, i]) for i in range(3)]
    for copy in fetch:
        copy.start()
    for i in range(3):
        fetch[i].wait()
        store[i].start()
    for copy in store:
        copy.wait()


def layer(dims, tokens, slot_params, w_up, w_down, cotangent):
    ny, nx, nz, zl = dims
    nyx, zh = ny * nx, nz // zl
    experts = nyx * nz
    seq, feat = tokens.shape
    columns = slot_params.shape[1]
    depth, hidden = w_up.shape[1:]
    lanes = feat // 2
    vmem, dma = pltpu.VMEM, pltpu.SemaphoreType.DMA
    piece = feat // (nyx * zl)
    scratch = [
        vmem((2, seq, feat), BF16),
        vmem((feat, columns), BF16),
        vmem((2, seq, feat), BF16),
        vmem((depth, hidden), BF16),
        vmem((hidden, depth), BF16),
        dma((5,)),
        vmem((2, 2, seq, feat), F32),
        vmem((2, seq, feat), F32),
        vmem((seq, feat), BF16),
        vmem((seq, feat), BF16),
        vmem((feat, columns), F32),
        dma((3,)),
        dma((2,)),
        dma((2,)),
        vmem((2, feat, experts), BF16),
        vmem((2, feat, experts), BF16),
        dma((4,)),
        dma((4,)),
        vmem((seq, experts), F32),
        vmem((seq, experts), F32),
        vmem((2, seq, experts), F32),
        dma((2,)),
        dma((2,)),
        vmem((seq, experts), F32),
        vmem((seq, experts), F32),
        vmem((seq, experts), BF16),
        vmem((seq, experts), BF16),
        vmem((8 * experts, lanes), F32),
        vmem((2, nz, nyx, 4, lanes), BF16),
        vmem((2, 2, nz, nyx, 4, lanes), BF16),
        vmem((2, 2, 2, nyx, nz, 4, lanes), BF16),
        vmem((2, 2, nyx, nz, 4, lanes), BF16),
        vmem((2, nz, nyx, 4, lanes), BF16),
        dma((2, 2, 2)),
        dma((2, 2, 2)),
        vmem((2, 2, 2, 2, experts, feat), BF16),
        dma((2,)),
        dma((2,)),
        vmem((2, experts, hidden), F32),
        vmem((2, 2, experts, hidden), BF16),
        vmem((2, 2, 4, experts, feat), BF16),
        vmem((2, 4, experts, feat), BF16),
        dma((2, 2)),
        dma((2, 2)),
        vmem((2, 2, experts, feat), BF16),
        vmem((2, seq, experts), BF16),
        vmem((2, seq, experts), BF16),
        dma((2,)),
        dma((2,)),
        vmem((seq, experts), F32),
        vmem((seq, experts), F32),
        vmem((nyx * zl, 2, piece, experts), BF16),
        vmem((nyx * zl, 2, piece, experts), BF16),
        vmem((2, piece, experts), BF16),
        vmem((nz, 2, piece, experts), BF16),
        vmem((2, zl, piece, experts), BF16),
        vmem((2, nyx, zl, piece, experts), BF16),
        dma((3,)),
        dma((3,)),
        pltpu.SemaphoreType.REGULAR,
        pltpu.SemaphoreType.REGULAR,
        pltpu.SemaphoreType.REGULAR((2,)),
    ]
    hbm = pl.BlockSpec(memory_space=pltpu.HBM)
    results = pl.pallas_call(
        functools.partial(kernel, dims),
        out_shape=(
            jax.ShapeDtypeStruct((seq, feat), BF16),
            jax.ShapeDtypeStruct((seq, feat), BF16),
            jax.ShapeDtypeStruct((feat, columns), F32),
        ),
        in_specs=[hbm] * 5,
        out_specs=(hbm, hbm, hbm),
        scratch_shapes=scratch,
        compiler_params=pltpu.CompilerParams(
            collective_id=0, has_side_effects=True, vmem_limit_bytes=67043328
        ),
    )(tokens, slot_params, w_up[0], w_down[0], cotangent)
    mixed, grad_tokens, grad_params = pl.pallas_call(
        publish,
        out_shape=tuple(jax.ShapeDtypeStruct(r.shape, r.dtype) for r in results),
        in_specs=[hbm] * 3,
        out_specs=(hbm, hbm, hbm),
        scratch_shapes=[vmem(r.shape, r.dtype) for r in results] + [dma((2, 3))],
        compiler_params=pltpu.CompilerParams(vmem_limit_bytes=67043328),
    )(*results)
    return mixed, grad_tokens, grad_params


def build(mesh, dims):
    in_specs = (
        P(EXPERT, HALF),
        P(HALF, None),
        P(EXPERT, None, HALF),
        P(EXPERT, HALF, None),
        P(EXPERT, HALF),
    )
    out_specs = (P(EXPERT, HALF), P(EXPERT, HALF), P(HALF, None))
    return jax.shard_map(
        functools.partial(layer, dims),
        mesh=mesh,
        in_specs=in_specs,
        out_specs=out_specs,
        check_vma=False,
    )


def solution(mesh):
    return build(
        jax.sharding.Mesh(mesh.devices.reshape(4, 2, 16, 2, 2), EXPERT + HALF), (4, 2, 16, 4)
    )
```
